32 devices in a mesh: ra: 8 (over z, y), dec: 4 (over x, core).
Axes of the slice: x: 2, y: 2, z: 4, core: 2. Of those that a mesh axis runs over, the one named last changes fastest.
Arguments:
- start_block: float32 [64, 512, 128], P('ra', 'dec'), may hold values from -6 to 6
- edge_blocks: float32 [64, 4, 4, 132, 128], P('ra', 'dec'), may hold values from -0.25 to 0.25
- block_offsets: int32 [64, 4, 4], P('ra', 'dec'), may hold values from 0 to 4
- degree_counts: int32 [64, 512], P('ra', 'dec'), may hold values from 4 to 12
Outputs:
- basis: float32 [64, 512, 128], P('ra', 'dec')
- rfactor: float32 [128, 128], replicated
The draws below stay inside these ranges and needn't reach their ends.
All inputs are finite; a program needn't handle non-finite values.
Results may differ from the reference program's by a relative error of at most 0.0003.
Values sent between devices are 32-bit elements; how exact they have to be, the bound alone decides.
A program may use at most 64 MiB of HBM per device.

```python
import math
import jax
import jax.numpy as jnp
from jax import lax

CDEC = 128
COLS = 128
NBK = 4
NRA = 64
NDEC = 512
NODES = 32768
N_DEC = 4


def draw_start_block(key, part):
    key_common = jax.random.fold_in(key, 11)
    key_noise = jax.random.fold_in(key, 12)
    key_spread = jax.random.fold_in(key, 13)
    key_load = jax.random.fold_in(key, 16)
    key_load_signs = jax.random.fold_in(key, 17)
    spread = jnp.exp(jax.random.uniform(key_spread, (COLS,), jnp.float32, math.log(0.004), math.log(0.5)))
    load_signs = jnp.where(jax.random.bernoulli(key_load_signs, 0.5, (COLS,)), 1.0, -1.0).astype(jnp.float32)
    loadings = load_signs * jax.random.uniform(key_load, (COLS,), jnp.float32, 0.5, 1.5)
    common = jnp.clip(jax.random.normal(key_common, (NRA, NDEC, 1), jnp.float32), -2.5, 2.5)
    noise = jnp.clip(jax.random.normal(key_noise, (NRA, NDEC, COLS), jnp.float32), -3.0, 3.0)
    field = loadings * common + spread * noise
    return field.astype(jnp.float32)


def plant(values, own_key, least, high):
    dims = values.shape
    place = [jax.random.randint(jax.random.fold_in(own_key, axis), (), 0, dims[axis]) for axis in range(len(dims))]
    values = values.at[tuple(place)].set(least)
    longest = dims.index(max(dims))
    place[longest] = (place[longest] + 1) % dims[longest]
    return values.at[tuple(place)].set(high)


def block_levels(key, shape, pieces, smallest, largest):
    def one(dim, blocks):
        steps = jax.random.uniform(jax.random.fold_in(jax.random.fold_in(key, 6), dim), (blocks,), jnp.float32, smallest / len(pieces), largest / len(pieces))
        return jnp.repeat(jnp.exp(steps), shape[dim] // blocks).reshape((-1,) + (1,) * (len(shape) - dim - 1))

    gain = one(*pieces[0])
    for cut in pieces[1:]:
        gain = gain * one(*cut)
    return gain


def centred(rng, shape, scale, reach, shards=(), held_as=jnp.bfloat16):
    gain = block_levels(rng, shape, shards, -0.22, 0.18) if shards else 1.0
    entries = jax.random.normal(rng, shape, jnp.float32) * scale * gain
    return jnp.minimum(jnp.maximum(entries, -reach), reach).astype(held_as)


def setup_inputs(seed: int = 0) -> dict:
    arg_keys = jax.random.split(jax.random.key(seed), 5)
    return {
        "start_block": draw_start_block(jax.random.fold_in(arg_keys[4], 71), 0),
        "edge_blocks": centred(arg_keys[1], (NRA, N_DEC, NBK, CDEC + 4, CDEC), (NBK * (CDEC + 4)) ** -0.5, 0.25, ((0, 8), (1, 4)), jnp.float32),
        "block_offsets": plant(jax.random.randint(arg_keys[2], (NRA, N_DEC, NBK), 0, 5), jax.random.fold_in(arg_keys[2], 1), 0, 4).astype(jnp.int32),
        "degree_counts": plant(jax.random.randint(arg_keys[3], (NRA, NDEC), 4, 13), jax.random.fold_in(arg_keys[3], 1), 4, 12).astype(jnp.int32),
    }


def apply_operator(field, edge_blocks, block_offsets, degree_counts):
    padded = jnp.pad(field, ((0, 0), (2, 2), (0, 0)))
    starts = (jnp.arange(N_DEC) * CDEC).astype(jnp.int32)

    def window(part, begin):
        return lax.dynamic_slice_in_dim(part, begin, CDEC + 4, 1)

    def one_row(items):
        row_index, row_offsets, row_blocks, row_degree, row_field = items
        source = (row_index + row_offsets - 2) % NRA
        picked = padded[source]
        windows = jax.vmap(window)(picked, starts)
        coupled = jnp.einsum('dkqp,dkqc->dpc', row_blocks, windows, precision=lax.Precision.HIGHEST)
        coupled = coupled.reshape(NDEC, COLS)
        return row_degree.astype(field.dtype)[:, None] * row_field - coupled
    row_ids = jnp.arange(NRA).astype(jnp.int32)
    return lax.map(one_row, (row_ids, block_offsets, edge_blocks, degree_counts, field))

def cholesky_pass(matrix):
    gram = jnp.dot(matrix.T, matrix, precision=lax.Precision.HIGHEST)
    lower = jnp.linalg.cholesky(gram)
    identity = jnp.eye(COLS, dtype=matrix.dtype)
    inverse_lower = jax.scipy.linalg.solve_triangular(lower, identity, lower=True)
    ortho = jnp.dot(matrix, inverse_lower.T, precision=lax.Precision.HIGHEST)
    return (ortho, lower.T)

def reference(start_block, edge_blocks, block_offsets, degree_counts):
    previous = start_block
    image = apply_operator(start_block, edge_blocks, block_offsets, degree_counts)
    current = (image - 8.0 * start_block) / 4.0
    for order_index in range(3):
        image = apply_operator(current, edge_blocks, block_offsets, degree_counts)
        following = 2.0 * (image - 8.0 * current) / 4.0 - previous
        previous = current
        current = following
    filtered = current.reshape(NODES, COLS)
    ortho_first, upper_first = cholesky_pass(filtered)
    ortho_second, upper_second = cholesky_pass(ortho_first)
    scale = jnp.sqrt(jnp.asarray(NODES, dtype=filtered.dtype))
    basis = (ortho_second * scale).reshape(NRA, NDEC, COLS)
    rfactor = jnp.dot(upper_second, upper_first, precision=lax.Precision.HIGHEST) / scale
    return (basis, rfactor)
```

```python
import functools

import jax
import jax.numpy as jnp
from jax import lax
from jax.experimental import pallas as pl
from jax.experimental.pallas import tpu as pltpu
from jax.sharding import PartitionSpec as P

MESH = pl.DeviceIdType.MESH
F32 = jnp.float32
BF16 = jnp.bfloat16
STEPS = 4
HALO = 64


def three_parts(value):
    first = value.astype(BF16)
    rest = value - first.astype(F32)
    second = rest.astype(BF16)
    third = (rest - second.astype(F32)).astype(BF16)
    return first, second, third


def dotT(a, b):
    return lax.dot_general(a, b, (((0,), (0,)), ((), ())), preferred_element_type=F32)


def dot(a, b):
    return jnp.dot(a, b, preferred_element_type=F32)

def two_sum(a, b):
    total = a + b
    other = total - a
    return total, (a - (total - other)) + (b - other)


def slices(value):
    shift = jnp.max(jnp.abs(value), axis=0, keepdims=True) * (1.5 * 2.0**16)
    parts = []
    for _ in range(3):
        part = (value + shift) - shift
        value = value - part
        shift = shift * 2.0**-8
        parts.append(part)
    return parts


def sliced_gram(parts):
    first, second, third = [p.astype(BF16) for p in parts]
    tall = jnp.concatenate([first, second, third], axis=1)
    wide = dotT(tall, jnp.concatenate([first, second], axis=1))
    thin = dotT(tall, third)
    return (
        wide[0:128, 0:128],
        wide[0:128, 128:256] + wide[128:256, 0:128],
        wide[128:256, 128:256] + (thin[0:128] + wide[256:384, 0:128]),
        thin[128:256] + wide[256:384, 128:256],
        thin[256:384],
    )


def local_gram(matrix):
    first, second, third, fourth, fifth = sliced_gram(slices(matrix))
    high, error = two_sum(first, second)
    high, more = two_sum(high, third)
    return high, (error + more) + (fourth + fifth)


def six_products(a, b, dims):
    ah, am, al = three_parts(a)
    bh, bm, bl = three_parts(b)
    left = jnp.concatenate([ah, ah, ah, am, am, al], axis=dims[0])
    right = jnp.concatenate([bh, bm, bl, bh, bm, bh], axis=dims[1])
    return lax.dot_general(left, right, (((dims[0],), (dims[1],)), ((), ())), preferred_element_type=F32)


def group_rows(dec_count):
    return 32 // dec_count


def group_count(ra_count, dec_count):
    return ra_count // group_rows(dec_count)


def group_place(ra_count, dec_count):
    return lax.rem(lax.axis_index("ra"), group_rows(dec_count)) * dec_count + lax.axis_index("dec")


def group_partners(ra_count, dec_count):
    first = lax.axis_index("ra") // group_rows(dec_count) * group_rows(dec_count)
    place = group_place(ra_count, dec_count)
    places = [lax.rem(place + step, 32) for step in range(1, 32)]
    return [(first + p // dec_count, lax.rem(p, dec_count)) for p in places]


def other_partners(ra_count, dec_count):
    rows = group_rows(dec_count)
    return [
        (lax.rem(lax.axis_index("ra") + rows * step, ra_count), lax.axis_index("dec"))
        for step in range(1, group_count(ra_count, dec_count))
    ]


def sum_tiles(ra_count, dec_count, tiles, total, came, other, send_sem, recv_sem):
    place = group_place(ra_count, dec_count)
    partners = group_partners(ra_count, dec_count)

    def copy(slot, source, target, device):
        return pltpu.make_async_remote_copy(
            src_ref=source, dst_ref=target, send_sem=send_sem.at[slot], recv_sem=recv_sem.at[slot],
            device_id=device, device_id_type=MESH,
        )

    def add(pieces):
        value, error = pieces[0], jnp.zeros((8, 128), F32)
        for piece in pieces[1:]:
            value, more = two_sum(value, piece)
            error = error + more
        high, low = two_sum(value[0:4], value[4:8] + (error[0:4] + error[4:8]))
        return jnp.concatenate([high, low], axis=0)

    scatter = [
        copy(step, tiles.at[lax.rem(place + step, 32)], came.at[step], partners[step - 1]) for step in range(1, 32)
    ]
    for c in scatter:
        c.start()
    for c in scatter:
        c.wait_recv()
    value = add([tiles[place]] + [came[step] for step in range(1, 32)])
    across = []
    if group_count(ra_count, dec_count) > 1:
        other[0] = value
        across = [
            copy(63 + step, other.at[0], other.at[step], device)
            for step, device in enumerate(other_partners(ra_count, dec_count), 1)
        ]
        for c in across:
            c.start()
        for c in across:
            c.wait_recv()
        value = add([other[step] for step in range(len(across) + 1)])
    total[place] = value
    gather = [copy(31 + step, total.at[place], total.at[place], partners[step - 1]) for step in range(1, 32)]
    for c in gather:
        c.start()
    for c in gather:
        c.wait_recv()
    for c in scatter + across + gather:
        c.wait_send()


def filter_kernel(
    ra_count, dec_count, offsets, start, edges, degrees, out, total,
    fields, low, high, left, right, wide, thin, wide_halo, thin_halo, edge_pair, edge_third, degree_cols,
    tiles, came, other, send_sem, recv_sem, group_send, group_recv,
):
    rows = start.shape[0]
    ra = lax.axis_index("ra")
    dec = lax.axis_index("dec")
    up = lax.rem(ra + 1, ra_count)
    down = lax.rem(ra + ra_count - 1, ra_count)
    has_left = dec > 0
    has_right = dec < dec_count - 1

    barrier = pltpu.get_barrier_semaphore()

    def greet(r, d):
        pl.semaphore_signal(barrier, inc=1, device_id=(r, d), device_id_type=MESH)

    greet(up, dec)
    greet(down, dec)

    @pl.when(has_left)
    def _():
        for r in (up, down, ra):
            greet(r, dec - 1)

    @pl.when(has_right)
    def _():
        for r in (up, down, ra):
            greet(r, dec + 1)

    count = 2 + 3 * jnp.where(has_left, 1, 0) + 3 * jnp.where(has_right, 1, 0)
    if ra_count > 2 * STEPS or dec_count > STEPS:
        far = group_partners(ra_count, dec_count) + other_partners(ra_count, dec_count)
        for r, d in far:
            greet(r, d)
        count = count + len(far)
    pl.semaphore_wait(barrier, count)

    def copy(version, slot, source, target, r, d):
        return pltpu.make_async_remote_copy(
            src_ref=source, dst_ref=target, send_sem=send_sem.at[version, slot], recv_sem=recv_sem.at[version, slot],
            device_id=(r, d), device_id_type=MESH,
        )

    def copies(version):
        field = start if version == 0 else fields.at[version - 1]
        first, last = pl.ds(0, 2), pl.ds(rows - 2, 2)
        head, tail = pl.ds(0, 8), pl.ds(120, 8)
        top, bottom, middle = pl.ds(0, 2), pl.ds(rows + 2, 2), pl.ds(2, rows)
        to_right, to_left = left.at[version], right.at[version]
        ring = [
            copy(version, 0, field.at[last], low.at[version], up, dec),
            copy(version, 1, field.at[first], high.at[version], down, dec),
        ]
        rightward = [
            copy(version, 2, field.at[last, tail], to_right.at[top], up, dec + 1),
            copy(version, 3, field.at[first, tail], to_right.at[bottom], down, dec + 1),
            copy(version, 4, field.at[:, tail], to_right.at[middle], ra, dec + 1),
        ]
        leftward = [
            copy(version, 5, field.at[last, head], to_left.at[top], up, dec - 1),
            copy(version, 6, field.at[first, head], to_left.at[bottom], down, dec - 1),
            copy(version, 7, field.at[:, head], to_left.at[middle], ra, dec - 1),
        ]
        return ring, rightward, leftward

    def start_edges(version):
        ring, rightward, leftward = copies(version)
        for c in ring:
            c.start()

        @pl.when(has_right)
        def _():
            for c in rightward[:2]:
                c.start()

        @pl.when(has_left)
        def _():
            for c in leftward[:2]:
                c.start()

    def start_middle(version):
        _, rightward, leftward = copies(version)

        @pl.when(has_right)
        def _():
            rightward[2].start()

        @pl.when(has_left)
        def _():
            leftward[2].start()

    def receive(version):
        ring, rightward, leftward = copies(version)
        for c in ring:
            c.wait_recv()

        @pl.when(has_left)
        def _():
            for c in rightward:
                c.wait_recv()

        @pl.when(has_right)
        def _():
            for c in leftward:
                c.wait_recv()

    def finish_sends(version):
        ring, rightward, leftward = copies(version)
        for c in ring:
            c.wait_send()

        @pl.when(has_right)
        def _():
            for c in rightward:
                c.wait_send()

        @pl.when(has_left)
        def _():
            for c in leftward:
                c.wait_send()

    def put(turn, place, value):
        first, second, third = three_parts(value)
        wide[turn, place, :, 0:128] = first
        wide[turn, place, :, 128:256] = second
        thin[turn, place] = third

    start_edges(0)
    start_middle(0)

    for version in range(STEPS):
        @pl.when(dec == 0)
        def _():
            left[version] = jnp.zeros_like(left[version])

        @pl.when(dec == dec_count - 1)
        def _():
            right[version] = jnp.zeros_like(right[version])

    turned = jnp.transpose(degrees[...].astype(F32))
    for row in range(rows):
        degree_cols[row] = jnp.broadcast_to(turned[:, row : row + 1], (128, 128)) - 8.0

    def prepare(row, carry):
        put(0, row + 2, start[row])
        pieces = [edges[row, k, 2:130, :].T for k in range(4)]
        blank = jnp.zeros((6, 128), F32)
        tips = []
        for k in range(4):
            tips += [blank, edges[row, k, 0:2, :], edges[row, k, 130:132, :], blank]
        pieces.append(jnp.concatenate(tips, axis=0).T)
        turned_edges = jnp.concatenate(pieces, axis=1)
        first, second, third = three_parts(turned_edges)
        edge_pair[row, 0:128] = first
        edge_pair[row, 128:256] = second
        edge_third[row] = third
        return carry

    lax.fori_loop(0, rows, prepare, 0)

    def one_row(version, row):
        turn = version % 2
        places = [row + offsets[row, k] for k in range(4)]
        both = jnp.concatenate([wide[turn, p] for p in places] + [wide_halo[p] for p in places], axis=0)
        last = jnp.concatenate([thin[turn, p] for p in places] + [thin_halo[p] for p in places], axis=0)
        pair = edge_pair[row]
        square = jnp.dot(pair, both, preferred_element_type=F32)
        small = jnp.dot(pair[0:128], last, preferred_element_type=F32) + jnp.dot(
            edge_third[row], both[:, 0:128], preferred_element_type=F32
        )
        small = square[128:256, 128:256] + small
        coupled = square[0:128, 0:128] + ((square[0:128, 128:256] + square[128:256, 0:128]) + small)
        field = start[row] if version == 0 else fields[version - 1, row]
        image = degree_cols[row] * field - coupled
        if version == 0:
            return image * 0.25
        before = start[row] if version == 1 else fields[version - 2, row]
        return image * 0.5 - before

    def run_row(version, row):
        value = one_row(version, row)
        if version == STEPS - 1:
            out[row] = value
        else:
            fields[version, row] = value
            put((version + 1) % 2, row + 2, value)

    for version in range(STEPS):
        turn = version % 2
        receive(version)
        for i in range(2):
            put(turn, i, low[version, i])
            put(turn, rows + 2 + i, high[version, i])

        def halo(place, carry):
            tips = jnp.concatenate([left[version, place], right[version, place]], axis=0)
            first, second, third = three_parts(tips)
            wide_halo[place, :, 0:128] = first
            wide_halo[place, :, 128:256] = second
            thin_halo[place] = third
            return carry

        lax.fori_loop(0, rows + 4, halo, 0)

        def boundary(i, carry):
            run_row(version, i + (rows - 4) * (i // 2))
            return carry

        def interior(i, carry):
            run_row(version, i + 2)
            return carry

        lax.fori_loop(0, 4, boundary, 0)
        if version < STEPS - 1:
            start_edges(version + 1)
        lax.fori_loop(0, rows - 4, interior, 0)
        if version < STEPS - 1:
            start_middle(version + 1)

    gram_high, gram_low = local_gram(out[...].reshape(rows * 128, 128))
    for m in range(16):
        for half in range(2):
            part = slice(8 * m + 4 * half, 8 * m + 4 * half + 4)
            tiles[2 * m + half] = jnp.concatenate([gram_high[part], gram_low[part]], axis=0)
    sum_tiles(ra_count, dec_count, tiles, total, came, other, group_send, group_recv)
    for version in range(STEPS):
        finish_sends(version)


def filtered_field(start_block, edges, offsets, degrees):
    rows = start_block.shape[0]
    vmem = pl.BlockSpec(memory_space=pltpu.VMEM)
    depth = 4 * 128 + HALO
    groups = group_count(lax.axis_size("ra"), lax.axis_size("dec"))
    return pl.pallas_call(
        functools.partial(filter_kernel, lax.axis_size("ra"), lax.axis_size("dec")),
        out_shape=(jax.ShapeDtypeStruct(start_block.shape, F32), jax.ShapeDtypeStruct((32, 8, 128), F32)),
        in_specs=[pl.BlockSpec(memory_space=pltpu.SMEM), vmem, vmem, vmem],
        out_specs=(vmem, vmem),
        scratch_shapes=[
            pltpu.VMEM((STEPS - 1, rows, 128, 128), F32),
            pltpu.VMEM((STEPS, 2, 128, 128), F32),
            pltpu.VMEM((STEPS, 2, 128, 128), F32),
            pltpu.VMEM((STEPS, rows + 4, 8, 128), F32),
            pltpu.VMEM((STEPS, rows + 4, 8, 128), F32),
            pltpu.VMEM((2, rows + 4, 128, 256), BF16),
            pltpu.VMEM((2, rows + 4, 128, 128), BF16),
            pltpu.VMEM((rows + 4, 16, 256), BF16),
            pltpu.VMEM((rows + 4, 16, 128), BF16),
            pltpu.VMEM((rows, 256, depth), BF16),
            pltpu.VMEM((rows, 128, depth), BF16),
            pltpu.VMEM((rows, 128, 128), F32),
            pltpu.VMEM((32, 8, 128), F32),
            pltpu.VMEM((32, 8, 128), F32),
            pltpu.VMEM((groups + 1, 8, 128), F32),
            pltpu.SemaphoreType.DMA((STEPS, 8)),
            pltpu.SemaphoreType.DMA((STEPS, 8)),
            pltpu.SemaphoreType.DMA((64 + groups,)),
            pltpu.SemaphoreType.DMA((64 + groups,)),
        ],
        compiler_params=pltpu.CompilerParams(collective_id=0, has_side_effects=True, vmem_limit_bytes=48 * 2**20),
        name="filter",
    )(offsets, start_block, edges, degrees)


TILE = (8, 128)


def row_of(value, i):
    return jnp.broadcast_to(value[i : i + 1], TILE)


def factor(gram, side0, panel=2):
    sub = lax.broadcasted_iota(jnp.int32, TILE, 0)
    lane = lax.broadcasted_iota(jnp.int32, TILE, 1)
    blocks = 16
    body = [gram[8 * m : 8 * m + 8] for m in range(blocks)]
    side = [side0[8 * m : 8 * m + 8] for m in range(blocks)]
    upper, inverse = [], []
    for start in range(0, blocks, panel):
        stop = start + panel
        for k in range(start, stop):
            columns = {
                m: [jnp.broadcast_to(body[m][:, 8 * k + i : 8 * k + i + 1], TILE) for i in range(8)] for m in range(k, stop)
            }
            left, right = body[k], side[k]
            left_rows, right_rows = [], []
            upper_rows, inverse_rows = left, right
            for i in range(8):
                root = row_of(lax.rsqrt(columns[k][i]), i)
                entries = [row_of(columns[k][j], i) * root for j in range(i + 1, 8)]
                for m in range(k, stop):
                    columns[m][i] = columns[m][i] * root
                    for j in range(i + 1, 8):
                        columns[m][j] = columns[m][j] - columns[m][i] * entries[j - i - 1]
                left_row, right_row = row_of(left, i) * root, row_of(right, i) * root
                left_rows.append(left_row)
                right_rows.append(right_row)
                upper_rows = jnp.where(sub == i, left_row, upper_rows)
                inverse_rows = jnp.where(sub == i, right_row, inverse_rows)
                if i < 7:
                    left = left - columns[k][i] * left_row
                    right = right - columns[k][i] * right_row
            upper.append(jnp.where(lane >= sub + 8 * k, upper_rows, 0.0))
            inverse.append(jnp.where(lane <= sub + 8 * k, inverse_rows, 0.0))
            for m in range(k + 1, stop):
                for i in range(8):
                    body[m] = body[m] - columns[m][i] * left_rows[i]
                    side[m] = side[m] - columns[m][i] * right_rows[i]
        if stop < blocks:
            u = jnp.concatenate(upper[start:stop], axis=0)
            v = jnp.concatenate(inverse[start:stop], axis=0)
            t = jnp.transpose(u)[8 * stop :]
            th, tm, tl = three_parts(t)
            wh, wm, wl = three_parts(jnp.concatenate([u, v], axis=1))
            left_parts = jnp.concatenate([th, th, th, tm, tm, tl], axis=1)
            right_parts = jnp.concatenate([wh, wm, wl, wh, wm, wh], axis=0)
            change = dot(left_parts, right_parts)
            for m in range(stop, blocks):
                body[m] = body[m] - change[8 * (m - stop) : 8 * (m - stop) + 8, 0:128]
                side[m] = side[m] - change[8 * (m - stop) : 8 * (m - stop) + 8, 128:256]
    return jnp.concatenate(upper, axis=0), jnp.concatenate(inverse, axis=0)


def identity():
    shape = (128, 128)
    return jnp.where(lax.broadcasted_iota(jnp.int32, shape, 0) == lax.broadcasted_iota(jnp.int32, shape, 1), 1.0, 0.0).astype(F32)


def two_factors(high, low):
    first, first_inverse = factor(high, identity())
    parts = slices(first)
    first = (parts[0] + parts[1]) + parts[2]
    terms = sliced_gram(parts)
    value, error = two_sum(high, -terms[0])
    value, more = two_sum(value, -terms[1])
    value, last = two_sum(value, -terms[2])
    rest = value + (((low + error) + (more + last)) - (terms[3] + terms[4]))
    gram_second = identity() + six_products(six_products(first_inverse, rest, (1, 0)), first_inverse, (1, 1))
    second, inverse = factor(gram_second, first_inverse)
    return six_products(second, first, (1, 0)), inverse


def finish_kernel(scale, gram, matrix, basis, rfactor):
    high = jnp.concatenate([gram[q, 0:4] for q in range(32)], axis=0)
    low = jnp.concatenate([gram[q, 4:8] for q in range(32)], axis=0)
    upper, inverse = two_factors(high, low)
    rfactor[...] = upper / scale
    basis[...] = six_products(matrix[...], inverse * scale, (1, 1))


def on_device(start_block, edge_blocks, block_offsets, degree_counts):
    current, gram = filtered_field(start_block, edge_blocks[:, 0], block_offsets[:, 0], degree_counts)
    row_count, node_count, column_count = current.shape
    filtered = current.reshape(row_count * node_count, column_count)
    total_nodes = row_count * node_count * lax.axis_size("ra") * lax.axis_size("dec")
    scale = total_nodes**0.5
    vmem = pl.BlockSpec(memory_space=pltpu.VMEM)
    basis, rfactor = pl.pallas_call(
        functools.partial(finish_kernel, scale),
        out_shape=(jax.ShapeDtypeStruct(filtered.shape, F32), jax.ShapeDtypeStruct((128, 128), F32)),
        in_specs=[vmem] * 2,
        out_specs=(vmem,) * 2,
        name="finish",
    )(gram, filtered)
    return (basis.reshape(current.shape), rfactor)


def solution(mesh):
    placed = (
        P("ra", "dec", None),
        P("ra", "dec", None, None, None),
        P("ra", "dec", None),
        P("ra", "dec"),
    )
    return jax.shard_map(
        on_device,
        mesh=mesh,
        in_specs=placed,
        out_specs=(P("ra", "dec", None), P()),
        check_vma=False,
    )
```

```python
import functools

import jax
import jax.numpy as jnp
from jax import lax
from jax.experimental import pallas as pl
from jax.experimental.pallas import tpu as pltpu
from jax.sharding import PartitionSpec as P

MESH = pl.DeviceIdType.MESH
F32 = jnp.float32
BF16 = jnp.bfloat16
STEPS = 4
HALO = 64


def three_parts(value):
    first = value.astype(BF16)
    rest = value - first.astype(F32)
    second = rest.astype(BF16)
    third = (rest - second.astype(F32)).astype(BF16)
    return first, second, third


def dotT(a, b):
    return lax.dot_general(a, b, (((0,), (0,)), ((), ())), preferred_element_type=F32)


def dotN(a, b):
    return lax.dot_general(a, b, (((1,), (1,)), ((), ())), preferred_element_type=F32)


def dot(a, b):
    return jnp.dot(a, b, preferred_element_type=F32)

def two_sum(a, b):
    total = a + b
    other = total - a
    return total, (a - (total - other)) + (b - other)


def slices(value, axis, rest):
    shift = jnp.max(jnp.abs(value), axis=axis, keepdims=True) * (1.5 * 2.0**16)
    parts = []
    for _ in range(3):
        part = (value + shift) - shift
        value = value - part
        shift = shift * 2.0**-8
        parts.append(part.astype(BF16))
    return parts + [value.astype(BF16)] if rest else parts


def squares(matrix):
    return [
        [matrix[i : i + 128, j : j + 128] for j in range(0, matrix.shape[1], 128)] for i in range(0, matrix.shape[0], 128)
    ]


def local_gram(matrix):
    one, two, three = slices(matrix, 0, False)
    tall = jnp.concatenate([one, two, three], axis=1)
    p = squares(dotT(tall, jnp.concatenate([one, two], axis=1)))
    q = squares(dotT(tall, three))
    high, error = two_sum(p[0][0], p[0][1] + p[1][0])
    high, more = two_sum(high, p[1][1] + (q[0][0] + p[2][0]))
    return high, (error + more) + ((q[1][0] + p[2][1]) + q[2][0])


def six_products(a, b, dims):
    ah, am, al = three_parts(a)
    bh, bm, bl = three_parts(b)
    left = jnp.concatenate([ah, ah, ah, am, am, al], axis=dims[0])
    right = jnp.concatenate([bh, bm, bl, bh, bm, bh], axis=dims[1])
    return lax.dot_general(left, right, (((dims[0],), (dims[1],)), ((), ())), preferred_element_type=F32)


def group_rows(dec_count):
    return 32 // dec_count


def group_count(ra_count, dec_count):
    return ra_count // group_rows(dec_count)


def group_place(ra_count, dec_count):
    return lax.rem(lax.axis_index("ra"), group_rows(dec_count)) * dec_count + lax.axis_index("dec")


def flip(value, mask):
    for bit in range(5):
        if mask >> bit & 1:
            value = value + 2**bit - 2 ** (bit + 1) * lax.rem(value // 2**bit, 2)
    return value


def group_partners(ra_count, dec_count):
    first = lax.axis_index("ra") // group_rows(dec_count) * group_rows(dec_count)
    place = group_place(ra_count, dec_count)
    places = [flip(place, step) for step in range(1, 32)]
    return [(p, (first + p // dec_count, lax.rem(p, dec_count))) for p in places]


def other_partners(ra_count, dec_count):
    rows = group_rows(dec_count)
    return [
        (lax.rem(lax.axis_index("ra") + rows * step, ra_count), lax.axis_index("dec"))
        for step in range(1, group_count(ra_count, dec_count))
    ]


def sum_tiles(ra_count, dec_count, tiles, total, came, other, send_sem, recv_sem):
    place = group_place(ra_count, dec_count)
    partners = group_partners(ra_count, dec_count)

    def copy(phase, source, target, device):
        return pltpu.make_async_remote_copy(
            src_ref=source, dst_ref=target, send_sem=send_sem.at[phase], recv_sem=recv_sem.at[phase],
            device_id=device, device_id_type=MESH,
        )

    def wait(semaphore, whole):
        pltpu.make_async_copy(whole, whole, semaphore).wait()

    def add(pieces):
        pairs = [(piece, jnp.zeros((8, 128), F32)) for piece in pieces]
        while len(pairs) > 1:
            merged = []
            for (a, e), (b, f) in zip(pairs[0::2], pairs[1::2]):
                value, more = two_sum(a, b)
                merged.append((value, more + (e + f)))
            pairs = merged + pairs[len(merged) * 2 :]
        value, error = pairs[0]
        high, low = two_sum(value[0:4], value[4:8] + (error[0:4] + error[4:8]))
        return jnp.concatenate([high, low], axis=0)

    for step in range(31, 0, -1):
        owner, device = partners[step - 1]
        copy(0, tiles.at[owner], came.at[step - 1], device).start()
    wait(recv_sem.at[0], came)
    value = add([tiles[place]] + [came[step - 1] for step in range(1, 32)])
    if group_count(ra_count, dec_count) > 1:
        other[0] = value
        for step, device in enumerate(other_partners(ra_count, dec_count), 1):
            copy(1, other.at[0], other.at[step], device).start()
        wait(recv_sem.at[1], other.at[pl.ds(1, group_count(ra_count, dec_count) - 1)])
        value = add([other[step] for step in range(group_count(ra_count, dec_count))])
        wait(send_sem.at[1], other.at[pl.ds(1, group_count(ra_count, dec_count) - 1)])
    total[place] = value
    for step in range(31, 0, -1):
        copy(2, total.at[place], total.at[place], partners[step - 1][1]).start()
    wait(recv_sem.at[2], came)
    wait(send_sem.at[0], came)
    wait(send_sem.at[2], came)


def filter_kernel(
    ra_count, dec_count, offsets, start, edges, degrees, out, total,
    fields, halo, left, right, wide, thin, wide_halo, thin_halo, raw_edges, edge_pair, degree_cols, sums,
    tiles, came, other, edge_sem, send_sem, recv_sem, group_send, group_recv,
):
    rows = start.shape[0]
    ra = lax.axis_index("ra")
    dec = lax.axis_index("dec")
    up = lax.rem(ra + 1, ra_count)
    down = lax.rem(ra + ra_count - 1, ra_count)
    has_left = dec > 0
    has_right = dec < dec_count - 1
    near = lax.rem(ra, 2)

    load_edges = pltpu.make_async_copy(edges, raw_edges, edge_sem.at[0])
    load_edges.start()
    barrier = pltpu.get_barrier_semaphore()

    def greet(r, d):
        pl.semaphore_signal(barrier, inc=1, device_id=(r, d), device_id_type=MESH)

    greet(up, dec)
    greet(down, dec)

    @pl.when(has_left)
    def _():
        for r in (up, down, ra):
            greet(r, dec - 1)

    @pl.when(has_right)
    def _():
        for r in (up, down, ra):
            greet(r, dec + 1)

    count = 2 + 3 * jnp.where(has_left, 1, 0) + 3 * jnp.where(has_right, 1, 0)
    if ra_count > 2 * STEPS or dec_count > STEPS:
        far = [device for _, device in group_partners(ra_count, dec_count)] + other_partners(ra_count, dec_count)
        for r, d in far:
            greet(r, d)
        count = count + len(far)
    pl.semaphore_wait(barrier, count)

    def copy(version, slot, source, target, r, d):
        return pltpu.make_async_remote_copy(
            src_ref=source, dst_ref=target, send_sem=send_sem.at[version, slot], recv_sem=recv_sem.at[version, slot],
            device_id=(r, d), device_id_type=MESH,
        )

    def field_of(version):
        return start if version == 0 else fields.at[version - 1]

    def row_copies(version, toward, depth):
        field = field_of(version)
        row = (rows - 1 - depth) * (1 - toward) + depth * toward
        target = up * (1 - toward) + down * toward
        corner = (1 - depth) * (1 - toward) + (rows + 2 + depth) * toward
        head, tail = pl.ds(0, 8), pl.ds(120, 8)
        slot = 10 * toward + 5 * depth
        ring = copy(version, slot, field.at[row], halo.at[version, toward, depth], target, dec)
        rightward = [
            copy(version, slot + 1, field.at[row, tail], left.at[version, corner], target, dec + 1),
            copy(version, slot + 2, field.at[row, tail], left.at[version, row + 2], ra, dec + 1),
        ]
        leftward = [
            copy(version, slot + 3, field.at[row, head], right.at[version, corner], target, dec - 1),
            copy(version, slot + 4, field.at[row, head], right.at[version, row + 2], ra, dec - 1),
        ]
        return ring, rightward, leftward

    def middle_copies(version):
        field = field_of(version)
        inner, own = pl.ds(2, rows - 4), pl.ds(4, rows - 4)
        head, tail = pl.ds(0, 8), pl.ds(120, 8)
        return (
            copy(version, 20, field.at[inner, tail], left.at[version, own], ra, dec + 1),
            copy(version, 21, field.at[inner, head], right.at[version, own], ra, dec - 1),
        )

    def start_row(version, toward, depth):
        ring, rightward, leftward = row_copies(version, toward, depth)

        @pl.when(has_right)
        def _():
            rightward[0].start()

        @pl.when(has_left)
        def _():
            leftward[0].start()

        ring.start()

        @pl.when(has_right)
        def _():
            rightward[1].start()

        @pl.when(has_left)
        def _():
            leftward[1].start()

    def start_middle(version):
        rightward, leftward = middle_copies(version)

        @pl.when(has_right)
        def _():
            rightward.start()

        @pl.when(has_left)
        def _():
            leftward.start()

    def receive_tips(version):
        middle = middle_copies(version)
        copies = [row_copies(version, toward, depth) for toward in range(2) for depth in range(2)]

        @pl.when(has_left)
        def _():
            for c in copies:
                c[1][1].wait_recv()
            middle[0].wait_recv()

        @pl.when(has_right)
        def _():
            for c in copies:
                c[2][1].wait_recv()
            middle[1].wait_recv()

    def receive_row(version, toward, depth):
        ring, rightward, leftward = row_copies(version, toward, depth)
        ring.wait_recv()

        @pl.when(has_left)
        def _():
            rightward[0].wait_recv()

        @pl.when(has_right)
        def _():
            leftward[0].wait_recv()

        place = (1 - depth) * (1 - toward) + (rows + 2 + depth) * toward
        put(version % 2, place, halo[version, toward, depth])
        put_tips(version, place)

    def finish_sends(version):
        middle = middle_copies(version)
        copies = [row_copies(version, toward, depth) for toward in range(2) for depth in range(2)]
        for c in copies:
            c[0].wait_send()

        @pl.when(has_right)
        def _():
            for c in copies:
                c[1][0].wait_send()
                c[1][1].wait_send()
            middle[0].wait_send()

        @pl.when(has_left)
        def _():
            for c in copies:
                c[2][0].wait_send()
                c[2][1].wait_send()
            middle[1].wait_send()

    def put(turn, place, value):
        first, second, third = three_parts(value)
        wide[turn, place, :, 0:128] = first
        wide[turn, place, :, 128:256] = second
        thin[turn, place] = third

    def put_tips(version, place):
        tips = jnp.concatenate([left[version, place], right[version, place]], axis=0)
        first, second, third = three_parts(tips)
        wide_halo[place, :, 0:128] = first
        wide_halo[place, :, 128:256] = second
        thin_halo[place, :, 0:128] = third

    for depth in range(2):
        for toward in (1 - near, near):
            start_row(0, toward, depth)
    start_middle(0)

    for version in range(STEPS):
        @pl.when(dec == 0)
        def _():
            left[version] = jnp.zeros_like(left[version])

        @pl.when(dec == dec_count - 1)
        def _():
            right[version] = jnp.zeros_like(right[version])

    thin_halo[:, :, 128:256] = jnp.zeros((rows + 4, 16, 128), BF16)
    turned = jnp.transpose(degrees[...].astype(F32))
    for row in range(rows):
        degree_cols[row] = jnp.broadcast_to(turned[:, row : row + 1], (128, 128)) - 8.0

    load_edges.wait()

    def prepare(row, carry):
        put(0, row + 2, start[row])
        blank = jnp.zeros((6, 128), F32)
        tips = []
        for k in range(4):
            piece = raw_edges[row, pl.ds(8 + k, 128, 4), :].T
            first = piece.astype(BF16)
            place = slice(128 * k, 128 * k + 128)
            edge_pair[row, 0:128, place] = first
            edge_pair[row, 128:256, place] = (piece - first.astype(F32)).astype(BF16)
            tips += [blank] + [raw_edges[row, 4 * q + k : 4 * q + k + 1, :] for q in (0, 1, 130, 131)] + [blank]
        piece = jnp.concatenate(tips, axis=0).T
        first = piece.astype(BF16)
        second = (piece - first.astype(F32)).astype(BF16)
        edge_pair[row, 0:128, 512:640] = jnp.concatenate([first, first], axis=1)
        edge_pair[row, 128:256, 512:640] = jnp.concatenate([second, jnp.zeros_like(second)], axis=1)
        return carry

    lax.fori_loop(0, rows, prepare, 0)

    def one_row(version, row):
        turn = version % 2
        places = [row + offsets[k, row] for k in range(4)]
        both = jnp.concatenate(
            [wide[turn, p] for p in places] + [wide_halo[p] for p in places] + [thin_halo[p] for p in places], axis=0
        )
        last = jnp.concatenate([thin[turn, p] for p in places], axis=0)
        square = jnp.dot(edge_pair[row], both, preferred_element_type=F32)
        small = jnp.dot(edge_pair[row, 0:128, 0:512], last, preferred_element_type=F32)
        small = square[128:256, 128:256] + small
        coupled = square[0:128, 0:128] + ((square[0:128, 128:256] + square[128:256, 0:128]) + small)
        field = start[row] if version == 0 else fields[version - 1, row]
        image = degree_cols[row] * field - coupled
        if version == 0:
            return image * 0.25
        before = start[row] if version == 1 else fields[version - 2, row]
        return image * 0.5 - before

    def keep(version, row, value):
        if version == STEPS - 1:
            out[row] = value
        else:
            fields[version, row] = value
            put((version + 1) % 2, row + 2, value)

    def add_gram(values):
        gram_high, gram_low = local_gram(jnp.concatenate(values, axis=0))
        sums[0], error = two_sum(sums[0], gram_high)
        sums[1] = sums[1] + (gram_low + error)

    def run_pair(version, row):
        values = [one_row(version, row + i) for i in range(2)]
        for i, value in enumerate(values):
            keep(version, row + i, value)
        if version == STEPS - 1:
            add_gram(values)

    def run_edge(version, toward):
        outer, inner = (rows - 1) * (1 - toward), (rows - 2) * (1 - toward) + toward
        order = ((inner, 1), (outer, 0)) if version % 2 == 0 else ((outer, 0), (inner, 1))
        values = []
        for i, (row, depth) in enumerate(order):
            if version % 2 == 0:
                receive_row(version, 1 - toward, i)
            elif i == 0:
                receive_row(version, 1 - toward, 1)
                receive_row(version, 1 - toward, 0)
            values.append(one_row(version, row))
            keep(version, row, values[-1])
            if version < STEPS - 1:
                start_row(version + 1, toward, depth)
        if version == STEPS - 1:
            add_gram(values)

    sums[...] = jnp.zeros_like(sums)
    for version in range(STEPS):
        receive_tips(version)

        def tip(i, carry):
            put_tips(version, i + 2)
            return carry

        lax.fori_loop(0, rows, tip, 0)

        def interior(i, carry):
            run_pair(version, 2 * i + 2)
            return carry

        lax.fori_loop(0, (rows - 4) // 2, interior, 0)
        if version < STEPS - 1:
            start_middle(version + 1)

        def boundary(turn, carry):
            run_edge(version, turn + near - 2 * turn * near)
            return carry

        lax.fori_loop(0, 2, boundary, 0)

    for m in range(16):
        for half in range(2):
            part = pl.ds(8 * m + 4 * half, 4)
            tiles[2 * m + half, 0:4] = sums[0, part]
            tiles[2 * m + half, 4:8] = sums[1, part]
    sum_tiles(ra_count, dec_count, tiles, total, came, other, group_send, group_recv)
    for version in range(STEPS):
        finish_sends(version)


def filtered_field(start_block, edges, offsets, degrees):
    rows = start_block.shape[0]
    vmem = pl.BlockSpec(memory_space=pltpu.VMEM)
    depth = 4 * 128 + 2 * HALO
    groups = group_count(lax.axis_size("ra"), lax.axis_size("dec"))
    return pl.pallas_call(
        functools.partial(filter_kernel, lax.axis_size("ra"), lax.axis_size("dec")),
        out_shape=(jax.ShapeDtypeStruct(start_block.shape, F32), jax.ShapeDtypeStruct((32, 8, 128), F32)),
        in_specs=[pl.BlockSpec(memory_space=pltpu.SMEM), vmem, pl.BlockSpec(memory_space=pl.ANY), vmem],
        out_specs=(vmem, vmem),
        scratch_shapes=[
            pltpu.VMEM((STEPS - 1, rows, 128, 128), F32),
            pltpu.VMEM((STEPS, 2, 2, 128, 128), F32),
            pltpu.VMEM((STEPS, rows + 4, 8, 128), F32),
            pltpu.VMEM((STEPS, rows + 4, 8, 128), F32),
            pltpu.VMEM((2, rows + 4, 128, 256), BF16),
            pltpu.VMEM((2, rows + 4, 128, 128), BF16),
            pltpu.VMEM((rows + 4, 16, 256), BF16),
            pltpu.VMEM((rows + 4, 16, 256), BF16),
            pltpu.VMEM(edges.shape, F32),
            pltpu.VMEM((rows, 256, depth), BF16),
            pltpu.VMEM((rows, 128, 128), F32),
            pltpu.VMEM((2, 128, 128), F32),
            pltpu.VMEM((32, 8, 128), F32),
            pltpu.VMEM((31, 8, 128), F32),
            pltpu.VMEM((groups, 8, 128), F32),
            pltpu.SemaphoreType.DMA((1,)),
            pltpu.SemaphoreType.DMA((STEPS, 22)),
            pltpu.SemaphoreType.DMA((STEPS, 22)),
            pltpu.SemaphoreType.DMA((3,)),
            pltpu.SemaphoreType.DMA((3,)),
        ],
        compiler_params=pltpu.CompilerParams(collective_id=0, has_side_effects=True, vmem_limit_bytes=60 * 2**20),
        name="filter",
    )(offsets, start_block, edges, degrees)


TILE = (8, 128)


def row_of(value, i):
    return jnp.broadcast_to(value[i : i + 1], TILE)


def factor(gram, side):
    sub = lax.broadcasted_iota(jnp.int32, TILE, 0)
    lane = lax.broadcasted_iota(jnp.int32, TILE, 1)
    blocks, panel = 16, 2
    body = [gram[8 * m : 8 * m + 8] for m in range(blocks)]
    side = [side[8 * m : 8 * m + 8] for m in range(blocks)]
    upper, inverse = [], []
    for begin in range(0, blocks, panel):
        end = begin + panel
        reach = min(blocks, end + panel)
        for k in range(begin, end):
            columns = {
                m: [jnp.broadcast_to(body[m][:, 8 * k + i : 8 * k + i + 1], TILE) for i in range(8)] for m in range(k, reach)
            }
            left, right = body[k], side[k]
            left_rows, right_rows = [], []
            upper_rows, inverse_rows = left, right
            for i in range(8):
                root = row_of(lax.rsqrt(columns[k][i]), i)
                entries = [row_of(columns[k][j], i) * root for j in range(i + 1, 8)]
                for m in range(k, reach):
                    columns[m][i] = columns[m][i] * root
                    for j in range(i + 1, 8):
                        columns[m][j] = columns[m][j] - columns[m][i] * entries[j - i - 1]
                left_row, right_row = row_of(left, i) * root, row_of(right, i) * root
                left_rows.append(left_row)
                right_rows.append(right_row)
                upper_rows = jnp.where(sub == i, left_row, upper_rows)
                inverse_rows = jnp.where(sub == i, right_row, inverse_rows)
                if i < 7:
                    left = left - columns[k][i] * left_row
                    right = right - columns[k][i] * right_row
            upper.append(jnp.where(lane >= sub + 8 * k, upper_rows, 0.0))
            inverse.append(jnp.where(lane <= sub + 8 * k, inverse_rows, 0.0))
            for m in range(k + 1, reach):
                for i in range(8):
                    body[m] = body[m] - columns[m][i] * left_rows[i]
                    side[m] = side[m] - columns[m][i] * right_rows[i]
        if reach < blocks:
            done = jnp.concatenate(upper[begin:end], axis=0)
            first, second, third = three_parts(jnp.concatenate([done, jnp.concatenate(inverse[begin:end], axis=0)], axis=1))
            parts = [p[:, 0:128].astype(F32) for p in (first, second, third)]
            turned = jnp.transpose(jnp.concatenate([parts[p] for p in (0, 0, 0, 1, 1, 2)], axis=0))[8 * reach :].astype(BF16)
            change = dot(turned, jnp.concatenate([first, second, third, first, second, first], axis=0))
            for m in range(reach, blocks):
                place = slice(8 * (m - reach), 8 * (m - reach) + 8)
                body[m] = body[m] - change[place, 0:128]
                side[m] = side[m] - change[place, 128:256]
    return jnp.concatenate(upper, axis=0), jnp.concatenate(inverse, axis=0)


def identity():
    shape = (128, 128)
    return jnp.where(lax.broadcasted_iota(jnp.int32, shape, 0) == lax.broadcasted_iota(jnp.int32, shape, 1), 1.0, 0.0).astype(F32)


def two_factors(high, low):
    first, inverse = factor(high, identity())
    parts = slices(first, 0, True)
    p = squares(dotT(jnp.concatenate(parts, axis=1), jnp.concatenate(parts[0:2], axis=1)))
    q = squares(dotT(jnp.concatenate(parts[0:3], axis=1), jnp.concatenate(parts[2:4], axis=1)))
    value, error = two_sum(high, -p[0][0])
    value, more = two_sum(value, -(p[0][1] + p[1][0]))
    value, last = two_sum(value, -(p[1][1] + (q[0][0] + p[2][0])))
    small = ((q[1][0] + p[2][1]) + (q[0][1] + p[3][0])) + (q[2][0] + (q[1][1] + p[3][1]))
    left_gram = value + (((low + error) + (more + last)) - small)

    p = squares(dotN(jnp.concatenate(slices(inverse, 1, True), axis=0), jnp.concatenate(slices(first, 1, True), axis=0)))
    left_inverse = (p[0][0] + (p[0][1] + p[1][0])) + (p[1][1] + (p[0][2] + p[2][0]))
    left_inverse = left_inverse + ((p[0][3] + p[3][0]) + (p[1][2] + p[2][1])) + ((p[2][2] + p[1][3]) + p[3][1]) - identity()

    turned = six_products(inverse, left_gram, (1, 0))
    gram_second = six_products(
        jnp.concatenate([turned, left_inverse], axis=1), jnp.concatenate([inverse, left_inverse], axis=1), (1, 1)
    )
    gram_second = identity() + (gram_second + (left_inverse + left_inverse.T))
    second, inverse = factor(gram_second, inverse)
    return six_products(second, first, (1, 0)), inverse


def finish_kernel(scale, gram, matrix, basis, rfactor):
    high = jnp.concatenate([gram[q, 0:4] for q in range(32)], axis=0)
    low = jnp.concatenate([gram[q, 4:8] for q in range(32)], axis=0)
    upper, inverse = two_factors(high, low)
    rfactor[...] = upper / scale
    basis[...] = six_products(matrix[...], inverse * scale, (1, 1))


def on_device(start_block, edge_blocks, block_offsets, degree_counts):
    edges = jnp.transpose(edge_blocks[:, 0], (0, 2, 1, 3)).reshape(start_block.shape[0], -1, 128)
    current, gram = filtered_field(start_block, edges, jnp.transpose(block_offsets[:, 0]), degree_counts)
    row_count, node_count, column_count = current.shape
    filtered = current.reshape(row_count * node_count, column_count)
    total_nodes = row_count * node_count * lax.axis_size("ra") * lax.axis_size("dec")
    scale = total_nodes**0.5
    vmem = pl.BlockSpec(memory_space=pltpu.VMEM)
    basis, rfactor = pl.pallas_call(
        functools.partial(finish_kernel, scale),
        out_shape=(jax.ShapeDtypeStruct(filtered.shape, F32), jax.ShapeDtypeStruct((128, 128), F32)),
        in_specs=[vmem] * 2,
        out_specs=(vmem,) * 2,
        name="finish",
    )(gram, filtered)
    return (basis.reshape(current.shape), rfactor)


def solution(mesh):
    placed = (
        P("ra", "dec", None),
        P("ra", "dec", None, None, None),
        P("ra", "dec", None),
        P("ra", "dec"),
    )
    return jax.shard_map(
        on_device,
        mesh=mesh,
        in_specs=placed,
        out_specs=(P("ra", "dec", None), P()),
        check_vma=False,
    )
```

```python
import functools

import jax
import jax.numpy as jnp
from jax import lax
from jax.experimental import pallas as pl
from jax.experimental.pallas import tpu as pltpu
from jax.sharding import PartitionSpec as P

MESH = pl.DeviceIdType.MESH
F32 = jnp.float32
BF16 = jnp.bfloat16
STEPS = 4
HALO = 64


def three_parts(value):
    first = value.astype(BF16)
    rest = value - first.astype(F32)
    second = rest.astype(BF16)
    third = (rest - second.astype(F32)).astype(BF16)
    return first, second, third


def dotT(a, b):
    return lax.dot_general(a, b, (((0,), (0,)), ((), ())), preferred_element_type=F32)


def dotN(a, b):
    return lax.dot_general(a, b, (((1,), (1,)), ((), ())), preferred_element_type=F32)


def dot(a, b):
    return jnp.dot(a, b, preferred_element_type=F32)

def two_sum(a, b):
    total = a + b
    other = total - a
    return total, (a - (total - other)) + (b - other)


def slices(value, axis, rest):
    shift = jnp.max(jnp.abs(value), axis=axis, keepdims=True) * (1.5 * 2.0**16)
    parts = []
    for _ in range(3):
        part = (value + shift) - shift
        value = value - part
        shift = shift * 2.0**-8
        parts.append(part.astype(BF16))
    return parts + [value.astype(BF16)] if rest else parts


def squares(matrix):
    return [
        [matrix[i : i + 128, j : j + 128] for j in range(0, matrix.shape[1], 128)] for i in range(0, matrix.shape[0], 128)
    ]


def local_gram(matrix):
    one, two, three = slices(matrix, 0, False)
    tall = jnp.concatenate([one, two, three], axis=1)
    p = squares(dotT(tall, jnp.concatenate([one, two], axis=1)))
    q = squares(dotT(tall, three))
    high, error = two_sum(p[0][0], p[0][1] + p[1][0])
    high, more = two_sum(high, p[1][1] + (q[0][0] + p[2][0]))
    return high, (error + more) + ((q[1][0] + p[2][1]) + q[2][0])


def six_products(a, b, dims):
    ah, am, al = three_parts(a)
    bh, bm, bl = three_parts(b)
    left = jnp.concatenate([ah, ah, ah, am, am, al], axis=dims[0])
    right = jnp.concatenate([bh, bm, bl, bh, bm, bh], axis=dims[1])
    return lax.dot_general(left, right, (((dims[0],), (dims[1],)), ((), ())), preferred_element_type=F32)


def group_rows(dec_count):
    return 32 // dec_count


def group_count(ra_count, dec_count):
    return ra_count // group_rows(dec_count)


def group_place(ra_count, dec_count):
    return lax.rem(lax.axis_index("ra"), group_rows(dec_count)) * dec_count + lax.axis_index("dec")


def group_partners(ra_count, dec_count):
    ra, dec = lax.axis_index("ra"), lax.axis_index("dec")
    place = group_place(ra_count, dec_count)
    flips = [2**bit - 2 ** (bit + 1) * lax.rem(lax.div(place, 2**bit), 2) for bit in range(5)]
    partners = []
    for step in range(1, 32):
        other, r, d = place, ra, dec
        for bit in range(5):
            if step >> bit & 1:
                other = other + flips[bit]
                if 2**bit < dec_count:
                    d = d + flips[bit]
                else:
                    r = r + lax.div(flips[bit], dec_count)
        partners.append((other, (r, d)))
    return partners


def other_partners(ra_count, dec_count):
    rows = group_rows(dec_count)
    return [
        (lax.rem(lax.axis_index("ra") + rows * step, ra_count), lax.axis_index("dec"))
        for step in range(1, group_count(ra_count, dec_count))
    ]


def sum_tiles(ra_count, dec_count, tiles, total, came, other, send_sem, recv_sem):
    place = group_place(ra_count, dec_count)
    partners = group_partners(ra_count, dec_count)

    def copy(phase, source, target, device):
        return pltpu.make_async_remote_copy(
            src_ref=source, dst_ref=target, send_sem=send_sem.at[phase], recv_sem=recv_sem.at[phase],
            device_id=device, device_id_type=MESH,
        )

    def wait(semaphore, whole):
        pltpu.make_async_copy(whole, whole, semaphore).wait()

    def add(pieces):
        pairs = [(piece, jnp.zeros((8, 128), F32)) for piece in pieces]
        while len(pairs) > 1:
            merged = []
            for (a, e), (b, f) in zip(pairs[0::2], pairs[1::2]):
                value, more = two_sum(a, b)
                merged.append((value, more + (e + f)))
            pairs = merged + pairs[len(merged) * 2 :]
        value, error = pairs[0]
        high, low = two_sum(value[0:4], value[4:8] + (error[0:4] + error[4:8]))
        return jnp.concatenate([high, low], axis=0)

    for step in range(31, 0, -1):
        owner, device = partners[step - 1]
        copy(0, tiles.at[owner], came.at[step - 1], device).start()
    wait(recv_sem.at[0], came)
    value = add([tiles[place]] + [came[step - 1] for step in range(1, 32)])
    if group_count(ra_count, dec_count) > 1:
        other[0] = value
        for step, device in enumerate(other_partners(ra_count, dec_count), 1):
            copy(1, other.at[0], other.at[step], device).start()
        wait(recv_sem.at[1], other.at[pl.ds(1, group_count(ra_count, dec_count) - 1)])
        value = add([other[step] for step in range(group_count(ra_count, dec_count))])
        wait(send_sem.at[1], other.at[pl.ds(1, group_count(ra_count, dec_count) - 1)])
    total[place] = value
    for step in range(31, 0, -1):
        copy(2, total.at[place], total.at[place], partners[step - 1][1]).start()
    wait(recv_sem.at[2], came)
    wait(send_sem.at[0], came)
    wait(send_sem.at[2], came)


def filter_kernel(
    ra_count, dec_count, offsets_in, start_in, edges, degrees_in, filtered, total,
    offsets, start, degrees, out, fields, halo, left, right, wide, thin, wide_halo, thin_halo, raw_edges, edge_pair, degree_cols, sums,
    tiles, came, other, edge_sem, send_sem, recv_sem, group_send, group_recv,
):
    rows = start.shape[0]
    ra = lax.axis_index("ra")
    dec = lax.axis_index("dec")
    up = lax.rem(ra + 1, ra_count)
    down = lax.rem(ra + ra_count - 1, ra_count)
    has_left = dec > 0
    has_right = dec < dec_count - 1
    near = lax.rem(ra, 2)

    load_start = pltpu.make_async_copy(start_in, start, edge_sem.at[1])
    load_edges = pltpu.make_async_copy(edges, raw_edges, edge_sem.at[0])
    load_offsets = pltpu.make_async_copy(offsets_in, offsets, edge_sem.at[2])
    load_degrees = pltpu.make_async_copy(degrees_in, degrees, edge_sem.at[3])
    for c in (load_start, load_offsets, load_degrees, load_edges):
        c.start()
    barrier = pltpu.get_barrier_semaphore()

    def greet(r, d):
        pl.semaphore_signal(barrier, inc=1, device_id=(r, d), device_id_type=MESH)

    greet(up, dec)
    greet(down, dec)

    @pl.when(has_left)
    def _():
        for r in (up, down, ra):
            greet(r, dec - 1)

    @pl.when(has_right)
    def _():
        for r in (up, down, ra):
            greet(r, dec + 1)

    count = 2 + 3 * jnp.where(has_left, 1, 0) + 3 * jnp.where(has_right, 1, 0)
    if ra_count > 2 * STEPS or dec_count > STEPS:
        far = [device for _, device in group_partners(ra_count, dec_count)] + other_partners(ra_count, dec_count)
        for r, d in far:
            greet(r, d)
        count = count + len(far)
    load_start.wait()
    pl.semaphore_wait(barrier, count)

    def copy(version, slot, source, target, r, d):
        return pltpu.make_async_remote_copy(
            src_ref=source, dst_ref=target, send_sem=send_sem.at[version, slot], recv_sem=recv_sem.at[version, slot],
            device_id=(r, d), device_id_type=MESH,
        )

    def field_of(version):
        return start if version == 0 else fields.at[version - 1]

    def row_copies(version, toward, depth):
        field = field_of(version)
        row = (rows - 1 - depth) * (1 - toward) + depth * toward
        target = up * (1 - toward) + down * toward
        corner = (1 - depth) * (1 - toward) + (rows + 2 + depth) * toward
        head, tail = pl.ds(0, 8), pl.ds(120, 8)
        slot = 10 * toward + 5 * depth
        ring = copy(version, slot, field.at[row], halo.at[version, toward, depth], target, dec)
        rightward = [
            copy(version, slot + 1, field.at[row, tail], left.at[version, corner], target, dec + 1),
            copy(version, slot + 2, field.at[row, tail], left.at[version, row + 2], ra, dec + 1),
        ]
        leftward = [
            copy(version, slot + 3, field.at[row, head], right.at[version, corner], target, dec - 1),
            copy(version, slot + 4, field.at[row, head], right.at[version, row + 2], ra, dec - 1),
        ]
        return ring, rightward, leftward

    def middle_copies(version):
        field = field_of(version)
        inner, own = pl.ds(2, rows - 4), pl.ds(4, rows - 4)
        head, tail = pl.ds(0, 8), pl.ds(120, 8)
        return (
            copy(version, 20, field.at[inner, tail], left.at[version, own], ra, dec + 1),
            copy(version, 21, field.at[inner, head], right.at[version, own], ra, dec - 1),
        )

    def start_row(version, toward, depth):
        ring, rightward, leftward = row_copies(version, toward, depth)

        @pl.when(has_right)
        def _():
            rightward[0].start()

        @pl.when(has_left)
        def _():
            leftward[0].start()

        ring.start()

        @pl.when(has_right)
        def _():
            rightward[1].start()

        @pl.when(has_left)
        def _():
            leftward[1].start()

    def start_middle(version):
        rightward, leftward = middle_copies(version)

        @pl.when(has_right)
        def _():
            rightward.start()

        @pl.when(has_left)
        def _():
            leftward.start()

    def receive_tips(version):
        middle = middle_copies(version)
        copies = [row_copies(version, toward, depth) for toward in range(2) for depth in range(2)]

        @pl.when(has_left)
        def _():
            for c in copies:
                c[1][1].wait_recv()
            middle[0].wait_recv()

        @pl.when(has_right)
        def _():
            for c in copies:
                c[2][1].wait_recv()
            middle[1].wait_recv()

    def receive_row(version, toward, depth):
        ring, rightward, leftward = row_copies(version, toward, depth)
        ring.wait_recv()

        @pl.when(has_left)
        def _():
            rightward[0].wait_recv()

        @pl.when(has_right)
        def _():
            leftward[0].wait_recv()

        place = (1 - depth) * (1 - toward) + (rows + 2 + depth) * toward
        put(version % 2, place, halo[version, toward, depth])
        put_tips(version, place)

    def finish_sends(version):
        middle = middle_copies(version)
        copies = [row_copies(version, toward, depth) for toward in range(2) for depth in range(2)]
        for c in copies:
            c[0].wait_send()

        @pl.when(has_right)
        def _():
            for c in copies:
                c[1][0].wait_send()
                c[1][1].wait_send()
            middle[0].wait_send()

        @pl.when(has_left)
        def _():
            for c in copies:
                c[2][0].wait_send()
                c[2][1].wait_send()
            middle[1].wait_send()

    def put(turn, place, value):
        first, second, third = three_parts(value)
        wide[turn, place, :, 0:128] = first
        wide[turn, place, :, 128:256] = second
        thin[turn, place] = third

    def put_tips(version, place):
        tips = jnp.concatenate([left[version, place], right[version, place]], axis=0)
        first, second, third = three_parts(tips)
        wide_halo[place, :, 0:128] = first
        wide_halo[place, :, 128:256] = second
        thin_halo[place, :, 0:128] = third

    for depth in range(2):
        for toward in (1 - near, near):
            start_row(0, toward, depth)
    start_middle(0)

    for version in range(STEPS):
        @pl.when(dec == 0)
        def _():
            left[version] = jnp.zeros_like(left[version])

        @pl.when(dec == dec_count - 1)
        def _():
            right[version] = jnp.zeros_like(right[version])

    thin_halo[:, :, 128:256] = jnp.zeros((rows + 4, 16, 128), BF16)
    load_offsets.wait()
    load_degrees.wait()
    turned = jnp.transpose(degrees[...].astype(F32))
    for row in range(rows):
        degree_cols[row] = jnp.broadcast_to(turned[:, row : row + 1], (128, 128)) - 8.0

    load_edges.wait()

    def prepare(row, carry):
        put(0, row + 2, start[row])
        blank = jnp.zeros((6, 128), F32)
        tips = []
        for k in range(4):
            piece = raw_edges[row, pl.ds(8 + k, 128, 4), :].T
            first = piece.astype(BF16)
            place = slice(128 * k, 128 * k + 128)
            edge_pair[row, 0:128, place] = first
            edge_pair[row, 128:256, place] = (piece - first.astype(F32)).astype(BF16)
            tips += [blank] + [raw_edges[row, 4 * q + k : 4 * q + k + 1, :] for q in (0, 1, 130, 131)] + [blank]
        piece = jnp.concatenate(tips, axis=0).T
        first = piece.astype(BF16)
        second = (piece - first.astype(F32)).astype(BF16)
        edge_pair[row, 0:128, 512:640] = jnp.concatenate([first, first], axis=1)
        edge_pair[row, 128:256, 512:640] = jnp.concatenate([second, jnp.zeros_like(second)], axis=1)
        return carry

    lax.fori_loop(0, rows, prepare, 0)

    def one_row(version, row):
        turn = version % 2
        places = [row + offsets[k, row] for k in range(4)]
        both = jnp.concatenate(
            [wide[turn, p] for p in places] + [wide_halo[p] for p in places] + [thin_halo[p] for p in places], axis=0
        )
        last = jnp.concatenate([thin[turn, p] for p in places], axis=0)
        square = jnp.dot(edge_pair[row], both, preferred_element_type=F32)
        small = jnp.dot(edge_pair[row, 0:128, 0:512], last, preferred_element_type=F32)
        small = square[128:256, 128:256] + small
        coupled = square[0:128, 0:128] + ((square[0:128, 128:256] + square[128:256, 0:128]) + small)
        field = start[row] if version == 0 else fields[version - 1, row]
        image = degree_cols[row] * field - coupled
        if version == 0:
            return image * 0.25
        before = start[row] if version == 1 else fields[version - 2, row]
        return image * 0.5 - before

    def keep(version, row, value):
        if version == STEPS - 1:
            out[row] = value
        else:
            fields[version, row] = value
            put((version + 1) % 2, row + 2, value)

    def add_gram(values):
        gram_high, gram_low = local_gram(jnp.concatenate(values, axis=0))
        sums[0], error = two_sum(sums[0], gram_high)
        sums[1] = sums[1] + (gram_low + error)

    def run_pair(version, row):
        values = [one_row(version, row + i) for i in range(2)]
        for i, value in enumerate(values):
            keep(version, row + i, value)
        if version == STEPS - 1:
            add_gram(values)

    def run_edge(version, toward):
        outer, inner = (rows - 1) * (1 - toward), (rows - 2) * (1 - toward) + toward
        order = ((inner, 1), (outer, 0)) if version % 2 == 0 else ((outer, 0), (inner, 1))
        values = []
        for i, (row, depth) in enumerate(order):
            if version % 2 == 0:
                receive_row(version, 1 - toward, i)
            elif i == 0:
                receive_row(version, 1 - toward, 1)
                receive_row(version, 1 - toward, 0)
            values.append(one_row(version, row))
            keep(version, row, values[-1])
            if version < STEPS - 1:
                start_row(version + 1, toward, depth)
        if version == STEPS - 1:
            add_gram(values)

    sums[...] = jnp.zeros_like(sums)
    for version in range(STEPS):
        receive_tips(version)

        def tip(i, carry):
            put_tips(version, i + 2)
            return carry

        lax.fori_loop(0, rows, tip, 0)

        def interior(i, carry):
            run_pair(version, 2 * i + 2)
            return carry

        lax.fori_loop(0, (rows - 4) // 2, interior, 0)
        if version < STEPS - 1:
            start_middle(version + 1)

        def boundary(turn, carry):
            run_edge(version, turn + near - 2 * turn * near)
            return carry

        lax.fori_loop(0, 2, boundary, 0)

    save = pltpu.make_async_copy(out, filtered, edge_sem.at[0])
    save.start()
    for m in range(16):
        for half in range(2):
            part = pl.ds(8 * m + 4 * half, 4)
            tiles[2 * m + half, 0:4] = sums[0, part]
            tiles[2 * m + half, 4:8] = sums[1, part]
    sum_tiles(ra_count, dec_count, tiles, total, came, other, group_send, group_recv)
    save.wait()
    for version in range(STEPS):
        finish_sends(version)


def filtered_field(start_block, edges, offsets, degrees):
    rows = start_block.shape[0]
    vmem = pl.BlockSpec(memory_space=pltpu.VMEM)
    depth = 4 * 128 + 2 * HALO
    groups = group_count(lax.axis_size("ra"), lax.axis_size("dec"))
    return pl.pallas_call(
        functools.partial(filter_kernel, lax.axis_size("ra"), lax.axis_size("dec")),
        out_shape=(jax.ShapeDtypeStruct(start_block.shape, F32), jax.ShapeDtypeStruct((32, 8, 128), F32)),
        in_specs=[pl.BlockSpec(memory_space=pl.ANY)] * 4,
        out_specs=(pl.BlockSpec(memory_space=pl.ANY), vmem),
        scratch_shapes=[
            pltpu.SMEM(offsets.shape, jnp.int32),
            pltpu.VMEM(start_block.shape, F32),
            pltpu.VMEM(degrees.shape, jnp.int32),
            pltpu.VMEM(start_block.shape, F32),
            pltpu.VMEM((STEPS - 1, rows, 128, 128), F32),
            pltpu.VMEM((STEPS, 2, 2, 128, 128), F32),
            pltpu.VMEM((STEPS, rows + 4, 8, 128), F32),
            pltpu.VMEM((STEPS, rows + 4, 8, 128), F32),
            pltpu.VMEM((2, rows + 4, 128, 256), BF16),
            pltpu.VMEM((2, rows + 4, 128, 128), BF16),
            pltpu.VMEM((rows + 4, 16, 256), BF16),
            pltpu.VMEM((rows + 4, 16, 256), BF16),
            pltpu.VMEM(edges.shape, F32),
            pltpu.VMEM((rows, 256, depth), BF16),
            pltpu.VMEM((rows, 128, 128), F32),
            pltpu.VMEM((2, 128, 128), F32),
            pltpu.VMEM((32, 8, 128), F32),
            pltpu.VMEM((31, 8, 128), F32),
            pltpu.VMEM((groups, 8, 128), F32),
            pltpu.SemaphoreType.DMA((4,)),
            pltpu.SemaphoreType.DMA((STEPS, 22)),
            pltpu.SemaphoreType.DMA((STEPS, 22)),
            pltpu.SemaphoreType.DMA((3,)),
            pltpu.SemaphoreType.DMA((3,)),
        ],
        compiler_params=pltpu.CompilerParams(collective_id=0, has_side_effects=True, vmem_limit_bytes=60 * 2**20),
        name="filter",
    )(offsets, start_block, edges, degrees)


TILE = (8, 128)


def row_of(value, i):
    return jnp.broadcast_to(value[i : i + 1], TILE)


def factor(gram, side):
    sub = lax.broadcasted_iota(jnp.int32, TILE, 0)
    lane = lax.broadcasted_iota(jnp.int32, TILE, 1)
    blocks, panel = 16, 2
    body = [gram[8 * m : 8 * m + 8] for m in range(blocks)]
    side = [side[8 * m : 8 * m + 8] for m in range(blocks)]
    upper, inverse = [], []
    for begin in range(0, blocks, panel):
        end = begin + panel
        reach = min(blocks, end + panel)
        for k in range(begin, end):
            columns = {
                m: [jnp.broadcast_to(body[m][:, 8 * k + i : 8 * k + i + 1], TILE) for i in range(8)] for m in range(k, reach)
            }
            left, right = body[k], side[k]
            left_rows, right_rows = [], []
            upper_rows, inverse_rows = left, right
            for i in range(8):
                root = row_of(lax.rsqrt(columns[k][i]), i)
                entries = [row_of(columns[k][j], i) * root for j in range(i + 1, 8)]
                for m in range(k, reach):
                    columns[m][i] = columns[m][i] * root
                    for j in range(i + 1, 8):
                        columns[m][j] = columns[m][j] - columns[m][i] * entries[j - i - 1]
                left_row, right_row = row_of(left, i) * root, row_of(right, i) * root
                left_rows.append(left_row)
                right_rows.append(right_row)
                upper_rows = jnp.where(sub == i, left_row, upper_rows)
                inverse_rows = jnp.where(sub == i, right_row, inverse_rows)
                if i < 7:
                    left = left - columns[k][i] * left_row
                    right = right - columns[k][i] * right_row
            upper.append(jnp.where(lane >= sub + 8 * k, upper_rows, 0.0))
            inverse.append(jnp.where(lane <= sub + 8 * k, inverse_rows, 0.0))
            for m in range(k + 1, reach):
                for i in range(8):
                    body[m] = body[m] - columns[m][i] * left_rows[i]
                    side[m] = side[m] - columns[m][i] * right_rows[i]
        if reach < blocks:
            done = jnp.concatenate(upper[begin:end], axis=0)
            first, second, third = three_parts(jnp.concatenate([done, jnp.concatenate(inverse[begin:end], axis=0)], axis=1))
            parts = [p[:, 0:128].astype(F32) for p in (first, second, third)]
            turned = jnp.transpose(jnp.concatenate([parts[p] for p in (0, 0, 0, 1, 1, 2)], axis=0))[8 * reach :].astype(BF16)
            change = dot(turned, jnp.concatenate([first, second, third, first, second, first], axis=0))
            for m in range(reach, blocks):
                place = slice(8 * (m - reach), 8 * (m - reach) + 8)
                body[m] = body[m] - change[place, 0:128]
                side[m] = side[m] - change[place, 128:256]
    return jnp.concatenate(upper, axis=0), jnp.concatenate(inverse, axis=0)


def identity():
    shape = (128, 128)
    return jnp.where(lax.broadcasted_iota(jnp.int32, shape, 0) == lax.broadcasted_iota(jnp.int32, shape, 1), 1.0, 0.0).astype(F32)


def two_factors(high, low):
    first, inverse = factor(high, identity())
    parts = slices(first, 0, True)
    p = squares(dotT(jnp.concatenate(parts, axis=1), jnp.concatenate(parts[0:2], axis=1)))
    q = squares(dotT(jnp.concatenate(parts[0:3], axis=1), jnp.concatenate(parts[2:4], axis=1)))
    value, error = two_sum(high, -p[0][0])
    value, more = two_sum(value, -(p[0][1] + p[1][0]))
    value, last = two_sum(value, -(p[1][1] + (q[0][0] + p[2][0])))
    small = ((q[1][0] + p[2][1]) + (q[0][1] + p[3][0])) + (q[2][0] + (q[1][1] + p[3][1]))
    left_gram = value + (((low + error) + (more + last)) - small)

    p = squares(dotN(jnp.concatenate(slices(inverse, 1, True), axis=0), jnp.concatenate(slices(first, 1, True), axis=0)))
    left_inverse = (p[0][0] + (p[0][1] + p[1][0])) + (p[1][1] + (p[0][2] + p[2][0]))
    left_inverse = left_inverse + ((p[0][3] + p[3][0]) + (p[1][2] + p[2][1])) + ((p[2][2] + p[1][3]) + p[3][1]) - identity()

    turned = six_products(inverse, left_gram, (1, 0))
    gram_second = six_products(
        jnp.concatenate([turned, left_inverse], axis=1), jnp.concatenate([inverse, left_inverse], axis=1), (1, 1)
    )
    gram_second = identity() + (gram_second + (left_inverse + left_inverse.T))
    second, inverse = factor(gram_second, inverse)
    return six_products(second, first, (1, 0)), inverse


def finish_kernel(scale, gram, matrix, basis, rfactor):
    high = jnp.concatenate([gram[q, 0:4] for q in range(32)], axis=0)
    low = jnp.concatenate([gram[q, 4:8] for q in range(32)], axis=0)
    upper, inverse = two_factors(high, low)
    rfactor[...] = upper / scale
    basis[...] = six_products(matrix[...], inverse * scale, (1, 1))


def on_device(start_block, edge_blocks, block_offsets, degree_counts):
    edges = jnp.transpose(edge_blocks[:, 0], (0, 2, 1, 3)).reshape(start_block.shape[0], -1, 128)
    current, gram = filtered_field(start_block, edges, jnp.transpose(block_offsets[:, 0]), degree_counts)
    row_count, node_count, column_count = current.shape
    filtered = current.reshape(row_count * node_count, column_count)
    total_nodes = row_count * node_count * lax.axis_size("ra") * lax.axis_size("dec")
    scale = total_nodes**0.5
    vmem = pl.BlockSpec(memory_space=pltpu.VMEM)
    basis, rfactor = pl.pallas_call(
        functools.partial(finish_kernel, scale),
        out_shape=(jax.ShapeDtypeStruct(filtered.shape, F32), jax.ShapeDtypeStruct((128, 128), F32)),
        in_specs=[vmem] * 2,
        out_specs=(vmem,) * 2,
        name="finish",
    )(gram, filtered)
    return (basis.reshape(current.shape), rfactor)


def solution(mesh):
    placed = (
        P("ra", "dec", None),
        P("ra", "dec", None, None, None),
        P("ra", "dec", None),
        P("ra", "dec"),
    )
    return jax.shard_map(
        on_device,
        mesh=mesh,
        in_specs=placed,
        out_specs=(P("ra", "dec", None), P()),
        check_vma=False,
    )
```

```python
import functools

import jax
import jax.numpy as jnp
from jax import lax
from jax.experimental import pallas as pl
from jax.experimental.pallas import tpu as pltpu
from jax.sharding import PartitionSpec as P

MESH = pl.DeviceIdType.MESH
F32 = jnp.float32
BF16 = jnp.bfloat16
STEPS = 4
HALO = 64


def three_parts(value):
    first = value.astype(BF16)
    rest = value - first.astype(F32)
    second = rest.astype(BF16)
    third = (rest - second.astype(F32)).astype(BF16)
    return first, second, third


def dotT(a, b):
    return lax.dot_general(a, b, (((0,), (0,)), ((), ())), preferred_element_type=F32)


def dotN(a, b):
    return lax.dot_general(a, b, (((1,), (1,)), ((), ())), preferred_element_type=F32)


def dot(a, b):
    return jnp.dot(a, b, preferred_element_type=F32)

def two_sum(a, b):
    total = a + b
    other = total - a
    return total, (a - (total - other)) + (b - other)


def slices(value, axis, rest):
    shift = jnp.max(jnp.abs(value), axis=axis, keepdims=True) * (1.5 * 2.0**16)
    parts = []
    for _ in range(3):
        part = (value + shift) - shift
        value = value - part
        shift = shift * 2.0**-8
        parts.append(part.astype(BF16))
    return parts + [value.astype(BF16)] if rest else parts


def squares(matrix):
    return [
        [matrix[i : i + 128, j : j + 128] for j in range(0, matrix.shape[1], 128)] for i in range(0, matrix.shape[0], 128)
    ]


def local_gram(matrix):
    one, two, three = slices(matrix, 0, False)
    tall = jnp.concatenate([one, two, three], axis=1)
    p = squares(dotT(tall, jnp.concatenate([one, two], axis=1)))
    q = squares(dotT(tall, three))
    high, error = two_sum(p[0][0], p[0][1] + p[1][0])
    high, more = two_sum(high, p[1][1] + (q[0][0] + p[2][0]))
    return high, (error + more) + ((q[1][0] + p[2][1]) + q[2][0])


def six_products(a, b, dims):
    ah, am, al = three_parts(a)
    bh, bm, bl = three_parts(b)
    left = jnp.concatenate([ah, ah, ah, am, am, al], axis=dims[0])
    right = jnp.concatenate([bh, bm, bl, bh, bm, bh], axis=dims[1])
    return lax.dot_general(left, right, (((dims[0],), (dims[1],)), ((), ())), preferred_element_type=F32)


def group_rows(dec_count):
    return 32 // dec_count


def group_count(ra_count, dec_count):
    return ra_count // group_rows(dec_count)


def group_place(ra_count, dec_count):
    return lax.rem(lax.axis_index("ra"), group_rows(dec_count)) * dec_count + lax.axis_index("dec")


def group_partners(ra_count, dec_count):
    ra, dec = lax.axis_index("ra"), lax.axis_index("dec")
    place = group_place(ra_count, dec_count)
    flips = [2**bit - 2 ** (bit + 1) * lax.rem(lax.div(place, 2**bit), 2) for bit in range(5)]
    partners = []
    for step in range(1, 32):
        other, r, d = place, ra, dec
        for bit in range(5):
            if step >> bit & 1:
                other = other + flips[bit]
                if 2**bit < dec_count:
                    d = d + flips[bit]
                else:
                    r = r + lax.div(flips[bit], dec_count)
        partners.append((other, (r, d)))
    return partners


def other_partners(ra_count, dec_count):
    rows = group_rows(dec_count)
    return [
        (lax.rem(lax.axis_index("ra") + rows * step, ra_count), lax.axis_index("dec"))
        for step in range(1, group_count(ra_count, dec_count))
    ]


def sum_tiles(ra_count, dec_count, tiles, total, came, other, send_sem, recv_sem):
    place = group_place(ra_count, dec_count)
    partners = group_partners(ra_count, dec_count)

    def copy(phase, source, target, device):
        return pltpu.make_async_remote_copy(
            src_ref=source, dst_ref=target, send_sem=send_sem.at[phase], recv_sem=recv_sem.at[phase],
            device_id=device, device_id_type=MESH,
        )

    def wait(semaphore, whole):
        pltpu.make_async_copy(whole, whole, semaphore).wait()

    def add(pieces):
        pairs = [(piece, jnp.zeros((8, 128), F32)) for piece in pieces]
        while len(pairs) > 1:
            merged = []
            for (a, e), (b, f) in zip(pairs[0::2], pairs[1::2]):
                value, more = two_sum(a, b)
                merged.append((value, more + (e + f)))
            pairs = merged + pairs[len(merged) * 2 :]
        value, error = pairs[0]
        high, low = two_sum(value[0:4], value[4:8] + (error[0:4] + error[4:8]))
        return jnp.concatenate([high, low], axis=0)

    for step in range(31, 0, -1):
        owner, device = partners[step - 1]
        copy(0, tiles.at[owner], came.at[step - 1], device).start()
    wait(recv_sem.at[0], came)
    value = add([tiles[place]] + [came[step - 1] for step in range(1, 32)])
    if group_count(ra_count, dec_count) > 1:
        other[0] = value
        for step, device in enumerate(other_partners(ra_count, dec_count), 1):
            copy(1, other.at[0], other.at[step], device).start()
        wait(recv_sem.at[1], other.at[pl.ds(1, group_count(ra_count, dec_count) - 1)])
        value = add([other[step] for step in range(group_count(ra_count, dec_count))])
        wait(send_sem.at[1], other.at[pl.ds(1, group_count(ra_count, dec_count) - 1)])
    total[place] = value
    for step in range(31, 0, -1):
        copy(2, total.at[place], total.at[place], partners[step - 1][1]).start()
    wait(recv_sem.at[2], came)
    wait(send_sem.at[0], came)
    wait(send_sem.at[2], came)


def filter_kernel(
    ra_count, dec_count, offsets_in, start_in, edges, degrees_in, filtered, total,
    offsets, start, degrees, out, fields, halo, left, right, wide, thin, wide_halo, thin_halo, raw_edges, edge_pair, degree_cols, sums,
    tiles, came, other, edge_sem, send_sem, recv_sem, group_send, group_recv,
):
    rows = start.shape[0]
    ra = lax.axis_index("ra")
    dec = lax.axis_index("dec")
    up = lax.rem(ra + 1, ra_count)
    down = lax.rem(ra + ra_count - 1, ra_count)
    has_left = dec > 0
    has_right = dec < dec_count - 1
    near = lax.rem(ra, 2)

    load_start = pltpu.make_async_copy(start_in, start, edge_sem.at[1])
    load_edges = pltpu.make_async_copy(edges, raw_edges, edge_sem.at[0])
    load_offsets = pltpu.make_async_copy(offsets_in, offsets, edge_sem.at[2])
    load_degrees = pltpu.make_async_copy(degrees_in, degrees, edge_sem.at[3])
    for c in (load_start, load_offsets, load_degrees, load_edges):
        c.start()
    barrier = pltpu.get_barrier_semaphore()

    def greet(r, d):
        pl.semaphore_signal(barrier, inc=1, device_id=(r, d), device_id_type=MESH)

    greet(up, dec)
    greet(down, dec)

    @pl.when(has_left)
    def _():
        for r in (up, down, ra):
            greet(r, dec - 1)

    @pl.when(has_right)
    def _():
        for r in (up, down, ra):
            greet(r, dec + 1)

    count = 2 + 3 * jnp.where(has_left, 1, 0) + 3 * jnp.where(has_right, 1, 0)
    if ra_count > 2 * STEPS or dec_count > STEPS:
        far = [device for _, device in group_partners(ra_count, dec_count)] + other_partners(ra_count, dec_count)
        for r, d in far:
            greet(r, d)
        count = count + len(far)
    load_start.wait()
    pl.semaphore_wait(barrier, count)

    def copy(version, slot, source, target, r, d):
        return pltpu.make_async_remote_copy(
            src_ref=source, dst_ref=target, send_sem=send_sem.at[version, slot], recv_sem=recv_sem.at[version, slot],
            device_id=(r, d), device_id_type=MESH,
        )

    def field_of(version):
        return start if version == 0 else fields.at[version - 1]

    def row_copies(version, toward, depth):
        field = field_of(version)
        row = (rows - 1 - depth) * (1 - toward) + depth * toward
        target = up * (1 - toward) + down * toward
        corner = (1 - depth) * (1 - toward) + (rows + 2 + depth) * toward
        head, tail = pl.ds(0, 8), pl.ds(120, 8)
        slot = 10 * toward + 5 * depth
        ring = copy(version, slot, field.at[row], halo.at[version, toward, depth], target, dec)
        rightward = [
            copy(version, slot + 1, field.at[row, tail], left.at[version, corner], target, dec + 1),
            copy(version, slot + 2, field.at[row, tail], left.at[version, row + 2], ra, dec + 1),
        ]
        leftward = [
            copy(version, slot + 3, field.at[row, head], right.at[version, corner], target, dec - 1),
            copy(version, slot + 4, field.at[row, head], right.at[version, row + 2], ra, dec - 1),
        ]
        return ring, rightward, leftward

    def middle_copies(version):
        field = field_of(version)
        inner, own = pl.ds(2, rows - 4), pl.ds(4, rows - 4)
        head, tail = pl.ds(0, 8), pl.ds(120, 8)
        return (
            copy(version, 20, field.at[inner, tail], left.at[version, own], ra, dec + 1),
            copy(version, 21, field.at[inner, head], right.at[version, own], ra, dec - 1),
        )

    def start_row(version, toward, depth):
        ring, rightward, leftward = row_copies(version, toward, depth)

        @pl.when(has_right)
        def _():
            rightward[0].start()

        @pl.when(has_left)
        def _():
            leftward[0].start()

        ring.start()

        @pl.when(has_right)
        def _():
            rightward[1].start()

        @pl.when(has_left)
        def _():
            leftward[1].start()

    def start_middle(version):
        rightward, leftward = middle_copies(version)

        @pl.when(has_right)
        def _():
            rightward.start()

        @pl.when(has_left)
        def _():
            leftward.start()

    def receive_tips(version):
        middle = middle_copies(version)
        copies = [row_copies(version, toward, depth) for toward in range(2) for depth in range(2)]

        @pl.when(has_left)
        def _():
            for c in copies:
                c[1][1].wait_recv()
            middle[0].wait_recv()

        @pl.when(has_right)
        def _():
            for c in copies:
                c[2][1].wait_recv()
            middle[1].wait_recv()

    def receive_row(version, toward, depth):
        ring, rightward, leftward = row_copies(version, toward, depth)
        ring.wait_recv()

        @pl.when(has_left)
        def _():
            rightward[0].wait_recv()

        @pl.when(has_right)
        def _():
            leftward[0].wait_recv()

        place = (1 - depth) * (1 - toward) + (rows + 2 + depth) * toward
        put(version % 2, place, halo[version, toward, depth])
        put_tips(version, place)

    def finish_sends(version):
        middle = middle_copies(version)
        copies = [row_copies(version, toward, depth) for toward in range(2) for depth in range(2)]
        for c in copies:
            c[0].wait_send()

        @pl.when(has_right)
        def _():
            for c in copies:
                c[1][0].wait_send()
                c[1][1].wait_send()
            middle[0].wait_send()

        @pl.when(has_left)
        def _():
            for c in copies:
                c[2][0].wait_send()
                c[2][1].wait_send()
            middle[1].wait_send()

    def put(turn, place, value):
        first, second, third = three_parts(value)
        wide[turn, place, :, 0:128] = first
        wide[turn, place, :, 128:256] = second
        thin[turn, place] = third

    def put_tips(version, place):
        tips = jnp.concatenate([left[version, place], right[version, place]], axis=0)
        first, second, third = three_parts(tips)
        wide_halo[place, :, 0:128] = first
        wide_halo[place, :, 128:256] = second
        thin_halo[place, :, 0:128] = third

    for depth in range(2):
        for toward in (1 - near, near):
            start_row(0, toward, depth)
    start_middle(0)

    for version in range(STEPS):
        @pl.when(dec == 0)
        def _():
            left[version] = jnp.zeros_like(left[version])

        @pl.when(dec == dec_count - 1)
        def _():
            right[version] = jnp.zeros_like(right[version])

    thin_halo[:, :, 128:256] = jnp.zeros((rows + 4, 16, 128), BF16)
    load_offsets.wait()
    load_degrees.wait()
    turned = jnp.transpose(degrees[...].astype(F32))
    for row in range(rows):
        degree_cols[row] = jnp.broadcast_to(turned[:, row : row + 1], (128, 128)) - 8.0

    load_edges.wait()

    def prepare(row, carry):
        put(0, row + 2, start[row])
        blank = jnp.zeros((6, 128), F32)
        tips = []
        for k in range(4):
            piece = raw_edges[row, pl.ds(8 + k, 128, 4), :].T
            first = piece.astype(BF16)
            place = slice(128 * k, 128 * k + 128)
            edge_pair[row, 0:128, place] = first
            edge_pair[row, 128:256, place] = (piece - first.astype(F32)).astype(BF16)
            tips += [blank] + [raw_edges[row, 4 * q + k : 4 * q + k + 1, :] for q in (0, 1, 130, 131)] + [blank]
        piece = jnp.concatenate(tips, axis=0).T
        first = piece.astype(BF16)
        second = (piece - first.astype(F32)).astype(BF16)
        edge_pair[row, 0:128, 512:640] = jnp.concatenate([first, first], axis=1)
        edge_pair[row, 128:256, 512:640] = jnp.concatenate([second, jnp.zeros_like(second)], axis=1)
        return carry

    lax.fori_loop(0, rows, prepare, 0)

    def one_row(version, row):
        turn = version % 2
        places = [row + offsets[k, row] for k in range(4)]
        both = jnp.concatenate(
            [wide[turn, p] for p in places] + [wide_halo[p] for p in places] + [thin_halo[p] for p in places], axis=0
        )
        last = jnp.concatenate([thin[turn, p] for p in places], axis=0)
        square = jnp.dot(edge_pair[row], both, preferred_element_type=F32)
        small = jnp.dot(edge_pair[row, 0:128, 0:512], last, preferred_element_type=F32)
        small = square[128:256, 128:256] + small
        coupled = square[0:128, 0:128] + ((square[0:128, 128:256] + square[128:256, 0:128]) + small)
        field = start[row] if version == 0 else fields[version - 1, row]
        image = degree_cols[row] * field - coupled
        if version == 0:
            return image * 0.25
        before = start[row] if version == 1 else fields[version - 2, row]
        return image * 0.5 - before

    def keep(version, row, value):
        if version == STEPS - 1:
            out[row] = value
        else:
            fields[version, row] = value
            put((version + 1) % 2, row + 2, value)

    def add_gram(values):
        gram_high, gram_low = local_gram(jnp.concatenate(values, axis=0))
        sums[0], error = two_sum(sums[0], gram_high)
        sums[1] = sums[1] + (gram_low + error)

    def run_pair(version, row):
        values = [one_row(version, row + i) for i in range(2)]
        for i, value in enumerate(values):
            keep(version, row + i, value)
        if version == STEPS - 1:
            add_gram(values)

    def run_edge(version, toward):
        outer, inner = (rows - 1) * (1 - toward), (rows - 2) * (1 - toward) + toward
        order = ((inner, 1), (outer, 0)) if version % 2 == 0 else ((outer, 0), (inner, 1))
        values = []
        for i, (row, depth) in enumerate(order):
            if version % 2 == 0:
                receive_row(version, 1 - toward, i)
            elif i == 0:
                receive_row(version, 1 - toward, 1)
                receive_row(version, 1 - toward, 0)
            values.append(one_row(version, row))
            keep(version, row, values[-1])
            if version < STEPS - 1:
                start_row(version + 1, toward, depth)
        if version == STEPS - 1:
            add_gram(values)

    sums[...] = jnp.zeros_like(sums)
    for version in range(STEPS):
        receive_tips(version)

        def tip(i, carry):
            put_tips(version, i + 2)
            return carry

        lax.fori_loop(0, rows, tip, 0)

        def interior(i, carry):
            run_pair(version, 2 * i + 2)
            return carry

        lax.fori_loop(0, (rows - 4) // 2, interior, 0)
        if version < STEPS - 1:
            start_middle(version + 1)

        def boundary(turn, carry):
            run_edge(version, turn + near - 2 * turn * near)
            return carry

        lax.fori_loop(0, 2, boundary, 0)

    save = pltpu.make_async_copy(out, filtered, edge_sem.at[0])
    save.start()
    for m in range(16):
        for half in range(2):
            part = pl.ds(8 * m + 4 * half, 4)
            tiles[2 * m + half, 0:4] = sums[0, part]
            tiles[2 * m + half, 4:8] = sums[1, part]
    sum_tiles(ra_count, dec_count, tiles, total, came, other, group_send, group_recv)
    save.wait()
    for version in range(STEPS):
        finish_sends(version)


def filtered_field(start_block, edges, offsets, degrees):
    rows = start_block.shape[0]
    vmem = pl.BlockSpec(memory_space=pltpu.VMEM)
    depth = 4 * 128 + 2 * HALO
    groups = group_count(lax.axis_size("ra"), lax.axis_size("dec"))
    return pl.pallas_call(
        functools.partial(filter_kernel, lax.axis_size("ra"), lax.axis_size("dec")),
        out_shape=(jax.ShapeDtypeStruct(start_block.shape, F32), jax.ShapeDtypeStruct((32, 8, 128), F32)),
        in_specs=[pl.BlockSpec(memory_space=pl.ANY)] * 4,
        out_specs=(pl.BlockSpec(memory_space=pl.ANY), vmem),
        scratch_shapes=[
            pltpu.SMEM(offsets.shape, jnp.int32),
            pltpu.VMEM(start_block.shape, F32),
            pltpu.VMEM(degrees.shape, jnp.int32),
            pltpu.VMEM(start_block.shape, F32),
            pltpu.VMEM((STEPS - 1, rows, 128, 128), F32),
            pltpu.VMEM((STEPS, 2, 2, 128, 128), F32),
            pltpu.VMEM((STEPS, rows + 4, 8, 128), F32),
            pltpu.VMEM((STEPS, rows + 4, 8, 128), F32),
            pltpu.VMEM((2, rows + 4, 128, 256), BF16),
            pltpu.VMEM((2, rows + 4, 128, 128), BF16),
            pltpu.VMEM((rows + 4, 16, 256), BF16),
            pltpu.VMEM((rows + 4, 16, 256), BF16),
            pltpu.VMEM(edges.shape, F32),
            pltpu.VMEM((rows, 256, depth), BF16),
            pltpu.VMEM((rows, 128, 128), F32),
            pltpu.VMEM((2, 128, 128), F32),
            pltpu.VMEM((32, 8, 128), F32),
            pltpu.VMEM((31, 8, 128), F32),
            pltpu.VMEM((groups, 8, 128), F32),
            pltpu.SemaphoreType.DMA((4,)),
            pltpu.SemaphoreType.DMA((STEPS, 22)),
            pltpu.SemaphoreType.DMA((STEPS, 22)),
            pltpu.SemaphoreType.DMA((3,)),
            pltpu.SemaphoreType.DMA((3,)),
        ],
        compiler_params=pltpu.CompilerParams(collective_id=0, has_side_effects=True, vmem_limit_bytes=60 * 2**20),
        name="filter",
    )(offsets, start_block, edges, degrees)


TILE = (8, 128)


def row_of(value, i):
    return jnp.broadcast_to(value[i : i + 1], TILE)


def factor(gram, side):
    sub = lax.broadcasted_iota(jnp.int32, TILE, 0)
    lane = lax.broadcasted_iota(jnp.int32, TILE, 1)
    blocks, panel = 16, 2
    width = 8 * panel
    body = [gram[8 * m : 8 * m + 8] for m in range(blocks)]
    side = [side[8 * m : 8 * m + 8] for m in range(blocks)]
    upper, inverse = [], []
    for begin in range(0, blocks, panel):
        end = begin + panel
        reach = min(blocks, end + panel)
        columns = {
            m: [jnp.broadcast_to(body[m][:, 8 * begin + j : 8 * begin + j + 1], TILE) for j in range(width)]
            for m in range(begin, reach)
        }
        for i in range(width):
            k, s = begin + i // 8, i % 8
            root = row_of(lax.rsqrt(columns[k][i]), s)
            entries = {j: row_of(columns[k][j], s) * root for j in range(i + 1, width)}
            for m in range(k, reach):
                columns[m][i] = columns[m][i] * root
                for j in range(i + 1, width):
                    columns[m][j] = columns[m][j] - columns[m][i] * entries[j]
            left_row, right_row = row_of(body[k], s) * root, row_of(side[k], s) * root
            upper_rows = left_row if s == 0 else jnp.where(sub == s, left_row, upper_rows)
            inverse_rows = right_row if s == 0 else jnp.where(sub == s, right_row, inverse_rows)
            for m in range(k if s < 7 else k + 1, reach):
                body[m] = body[m] - columns[m][i] * left_row
                side[m] = side[m] - columns[m][i] * right_row
            if s == 7:
                upper.append(jnp.where(lane >= sub + 8 * k, upper_rows, 0.0))
                inverse.append(jnp.where(lane <= sub + 8 * k, inverse_rows, 0.0))
        if reach < blocks:
            done = jnp.concatenate(upper[begin:end], axis=0)
            first, second, third = three_parts(jnp.concatenate([done, jnp.concatenate(inverse[begin:end], axis=0)], axis=1))
            parts = [p[:, 0:128].astype(F32) for p in (first, second, third)]
            turned = jnp.transpose(jnp.concatenate([parts[p] for p in (0, 0, 0, 1, 1, 2)], axis=0))[8 * reach :].astype(BF16)
            change = dot(turned, jnp.concatenate([first, second, third, first, second, first], axis=0))
            for m in range(reach, blocks):
                place = slice(8 * (m - reach), 8 * (m - reach) + 8)
                body[m] = body[m] - change[place, 0:128]
                side[m] = side[m] - change[place, 128:256]
    return jnp.concatenate(upper, axis=0), jnp.concatenate(inverse, axis=0)


def identity():
    shape = (128, 128)
    return jnp.where(lax.broadcasted_iota(jnp.int32, shape, 0) == lax.broadcasted_iota(jnp.int32, shape, 1), 1.0, 0.0).astype(F32)


def two_factors(high, low):
    first, inverse = factor(high, identity())
    parts = slices(first, 0, True)
    p = squares(dotT(jnp.concatenate(parts, axis=1), jnp.concatenate(parts[0:2], axis=1)))
    q = squares(dotT(jnp.concatenate(parts[0:3], axis=1), jnp.concatenate(parts[2:4], axis=1)))
    value, error = two_sum(high, -p[0][0])
    value, more = two_sum(value, -(p[0][1] + p[1][0]))
    value, last = two_sum(value, -(p[1][1] + (q[0][0] + p[2][0])))
    small = ((q[1][0] + p[2][1]) + (q[0][1] + p[3][0])) + (q[2][0] + (q[1][1] + p[3][1]))
    left_gram = value + (((low + error) + (more + last)) - small)

    p = squares(dotN(jnp.concatenate(slices(inverse, 1, True), axis=0), jnp.concatenate(slices(first, 1, True), axis=0)))
    left_inverse = (p[0][0] + (p[0][1] + p[1][0])) + (p[1][1] + (p[0][2] + p[2][0]))
    left_inverse = left_inverse + ((p[0][3] + p[3][0]) + (p[1][2] + p[2][1])) + ((p[2][2] + p[1][3]) + p[3][1]) - identity()

    turned = six_products(inverse, left_gram, (1, 0))
    gram_second = six_products(
        jnp.concatenate([turned, left_inverse], axis=1), jnp.concatenate([inverse, left_inverse], axis=1), (1, 1)
    )
    gram_second = identity() + (gram_second + (left_inverse + left_inverse.T))
    second, inverse = factor(gram_second, inverse)
    return six_products(second, first, (1, 0)), inverse


def finish_kernel(scale, gram, matrix, basis, rfactor):
    high = jnp.concatenate([gram[q, 0:4] for q in range(32)], axis=0)
    low = jnp.concatenate([gram[q, 4:8] for q in range(32)], axis=0)
    upper, inverse = two_factors(high, low)
    rfactor[...] = upper / scale
    basis[...] = six_products(matrix[...], inverse * scale, (1, 1))


def on_device(start_block, edge_blocks, block_offsets, degree_counts):
    edges = jnp.transpose(edge_blocks[:, 0], (0, 2, 1, 3)).reshape(start_block.shape[0], -1, 128)
    current, gram = filtered_field(start_block, edges, jnp.transpose(block_offsets[:, 0]), degree_counts)
    row_count, node_count, column_count = current.shape
    filtered = current.reshape(row_count * node_count, column_count)
    total_nodes = row_count * node_count * lax.axis_size("ra") * lax.axis_size("dec")
    scale = total_nodes**0.5
    vmem = pl.BlockSpec(memory_space=pltpu.VMEM)
    basis, rfactor = pl.pallas_call(
        functools.partial(finish_kernel, scale),
        out_shape=(jax.ShapeDtypeStruct(filtered.shape, F32), jax.ShapeDtypeStruct((128, 128), F32)),
        in_specs=[vmem] * 2,
        out_specs=(vmem,) * 2,
        name="finish",
    )(gram, filtered)
    return (basis.reshape(current.shape), rfactor)


def solution(mesh):
    placed = (
        P("ra", "dec", None),
        P("ra", "dec", None, None, None),
        P("ra", "dec", None),
        P("ra", "dec"),
    )
    return jax.shard_map(
        on_device,
        mesh=mesh,
        in_specs=placed,
        out_specs=(P("ra", "dec", None), P()),
        check_vma=False,
    )
```

```python
import functools

import jax
import jax.numpy as jnp
from jax import lax
from jax.experimental import pallas as pl
from jax.experimental.pallas import tpu as pltpu
from jax.sharding import PartitionSpec as P

MESH = pl.DeviceIdType.MESH
F32 = jnp.float32
BF16 = jnp.bfloat16
STEPS = 4
HALO = 64


def three_parts(value):
    first = value.astype(BF16)
    rest = value - first.astype(F32)
    second = rest.astype(BF16)
    third = (rest - second.astype(F32)).astype(BF16)
    return first, second, third


def dotT(a, b):
    return lax.dot_general(a, b, (((0,), (0,)), ((), ())), preferred_element_type=F32)


def dotN(a, b):
    return lax.dot_general(a, b, (((1,), (1,)), ((), ())), preferred_element_type=F32)


def dot(a, b):
    return jnp.dot(a, b, preferred_element_type=F32)

def two_sum(a, b):
    total = a + b
    other = total - a
    return total, (a - (total - other)) + (b - other)


def slices(value, axis, rest):
    shift = jnp.max(jnp.abs(value), axis=axis, keepdims=True) * (1.5 * 2.0**16)
    parts = []
    for _ in range(3):
        part = (value + shift) - shift
        value = value - part
        shift = shift * 2.0**-8
        parts.append(part.astype(BF16))
    return parts + [value.astype(BF16)] if rest else parts


def squares(matrix):
    return [
        [matrix[i : i + 128, j : j + 128] for j in range(0, matrix.shape[1], 128)] for i in range(0, matrix.shape[0], 128)
    ]


def local_gram(matrix):
    one, two, three = slices(matrix, 0, False)
    tall = jnp.concatenate([one, two, three], axis=1)
    p = squares(dotT(tall, jnp.concatenate([one, two], axis=1)))
    q = squares(dotT(tall, three))
    high, error = two_sum(p[0][0], p[0][1] + p[1][0])
    high, more = two_sum(high, p[1][1] + (q[0][0] + p[2][0]))
    return high, (error + more) + ((q[1][0] + p[2][1]) + q[2][0])


def six_products(a, b, dims):
    ah, am, al = three_parts(a)
    bh, bm, bl = three_parts(b)
    left = jnp.concatenate([ah, ah, ah, am, am, al], axis=dims[0])
    right = jnp.concatenate([bh, bm, bl, bh, bm, bh], axis=dims[1])
    return lax.dot_general(left, right, (((dims[0],), (dims[1],)), ((), ())), preferred_element_type=F32)


def group_rows(dec_count):
    return 32 // dec_count


def group_count(ra_count, dec_count):
    return ra_count // group_rows(dec_count)


def group_place(ra_count, dec_count):
    return lax.rem(lax.axis_index("ra"), group_rows(dec_count)) * dec_count + lax.axis_index("dec")


def group_partners(ra_count, dec_count):
    ra, dec = lax.axis_index("ra"), lax.axis_index("dec")
    place = group_place(ra_count, dec_count)
    flips = [2**bit - 2 ** (bit + 1) * lax.rem(lax.div(place, 2**bit), 2) for bit in range(5)]
    partners = []
    for step in range(1, 32):
        other, r, d = place, ra, dec
        for bit in range(5):
            if step >> bit & 1:
                other = other + flips[bit]
                if 2**bit < dec_count:
                    d = d + flips[bit]
                else:
                    r = r + lax.div(flips[bit], dec_count)
        partners.append((other, (r, d)))
    return partners


def other_partners(ra_count, dec_count):
    rows = group_rows(dec_count)
    return [
        (lax.rem(lax.axis_index("ra") + rows * step, ra_count), lax.axis_index("dec"))
        for step in range(1, group_count(ra_count, dec_count))
    ]


def sum_tiles(ra_count, dec_count, tiles, total, came, other, send_sem, recv_sem):
    place = group_place(ra_count, dec_count)
    partners = group_partners(ra_count, dec_count)

    def copy(phase, source, target, device):
        return pltpu.make_async_remote_copy(
            src_ref=source, dst_ref=target, send_sem=send_sem.at[phase], recv_sem=recv_sem.at[phase],
            device_id=device, device_id_type=MESH,
        )

    def wait(semaphore, whole):
        pltpu.make_async_copy(whole, whole, semaphore).wait()

    def add(pieces):
        pairs = [(piece, jnp.zeros((8, 128), F32)) for piece in pieces]
        while len(pairs) > 1:
            merged = []
            for (a, e), (b, f) in zip(pairs[0::2], pairs[1::2]):
                value, more = two_sum(a, b)
                merged.append((value, more + (e + f)))
            pairs = merged + pairs[len(merged) * 2 :]
        value, error = pairs[0]
        high, low = two_sum(value[0:4], value[4:8] + (error[0:4] + error[4:8]))
        return jnp.concatenate([high, low], axis=0)

    for step in range(31, 0, -1):
        owner, device = partners[step - 1]
        copy(0, tiles.at[owner], came.at[step - 1], device).start()
    wait(recv_sem.at[0], came)
    value = add([tiles[place]] + [came[step - 1] for step in range(1, 32)])
    if group_count(ra_count, dec_count) > 1:
        other[0] = value
        for step, device in enumerate(other_partners(ra_count, dec_count), 1):
            copy(1, other.at[0], other.at[step], device).start()
        wait(recv_sem.at[1], other.at[pl.ds(1, group_count(ra_count, dec_count) - 1)])
        value = add([other[step] for step in range(group_count(ra_count, dec_count))])
        wait(send_sem.at[1], other.at[pl.ds(1, group_count(ra_count, dec_count) - 1)])
    total[place] = value
    for step in range(31, 0, -1):
        copy(2, total.at[place], total.at[place], partners[step - 1][1]).start()
    wait(recv_sem.at[2], came)
    wait(send_sem.at[0], came)
    wait(send_sem.at[2], came)


def filter_kernel(
    ra_count, dec_count, offsets_in, start_in, edges, degrees_in, filtered, total,
    offsets, start, degrees, out, fields, halo, left, right, wide, thin, wide_halo, thin_halo, raw_edges, edge_pair, degree_cols, sums,
    tiles, came, other, edge_sem, send_sem, recv_sem, group_send, group_recv,
):
    rows = start.shape[0]
    ra = lax.axis_index("ra")
    dec = lax.axis_index("dec")
    up = lax.rem(ra + 1, ra_count)
    down = lax.rem(ra + ra_count - 1, ra_count)
    has_left = dec > 0
    has_right = dec < dec_count - 1
    near = lax.rem(ra, 2)

    load_start = pltpu.make_async_copy(start_in, start, edge_sem.at[1])
    load_edges = pltpu.make_async_copy(edges, raw_edges, edge_sem.at[0])
    load_offsets = pltpu.make_async_copy(offsets_in, offsets, edge_sem.at[2])
    load_degrees = pltpu.make_async_copy(degrees_in, degrees, edge_sem.at[3])
    for c in (load_start, load_offsets, load_degrees, load_edges):
        c.start()
    barrier = pltpu.get_barrier_semaphore()

    def greet(r, d):
        pl.semaphore_signal(barrier, inc=1, device_id=(r, d), device_id_type=MESH)

    greet(up, dec)
    greet(down, dec)

    @pl.when(has_left)
    def _():
        for r in (up, down, ra):
            greet(r, dec - 1)

    @pl.when(has_right)
    def _():
        for r in (up, down, ra):
            greet(r, dec + 1)

    count = 2 + 3 * jnp.where(has_left, 1, 0) + 3 * jnp.where(has_right, 1, 0)
    if ra_count > 2 * STEPS or dec_count > STEPS:
        far = [device for _, device in group_partners(ra_count, dec_count)] + other_partners(ra_count, dec_count)
        for r, d in far:
            greet(r, d)
        count = count + len(far)
    load_start.wait()
    pl.semaphore_wait(barrier, count)

    def copy(version, slot, source, target, r, d):
        return pltpu.make_async_remote_copy(
            src_ref=source, dst_ref=target, send_sem=send_sem.at[version, slot], recv_sem=recv_sem.at[version, slot],
            device_id=(r, d), device_id_type=MESH,
        )

    def field_of(version):
        return start if version == 0 else fields.at[version - 1]

    def row_copies(version, toward, depth):
        field = field_of(version)
        row = (rows - 1 - depth) * (1 - toward) + depth * toward
        target = up * (1 - toward) + down * toward
        corner = (1 - depth) * (1 - toward) + (rows + 2 + depth) * toward
        slot = 10 * toward + 5 * depth
        ring = copy(version, slot, field.at[row], halo.at[version, toward, depth], target, dec)
        rightward = [
            copy(version, slot + 1, field.at[row, pl.ds(126, 2)], left.at[version, corner, pl.ds(6, 2)], target, dec + 1),
            copy(version, slot + 2, field.at[row, pl.ds(126, 2)], left.at[version, row + 2, pl.ds(6, 2)], ra, dec + 1),
        ]
        leftward = [
            copy(version, slot + 3, field.at[row, pl.ds(0, 2)], right.at[version, corner, pl.ds(0, 2)], target, dec - 1),
            copy(version, slot + 4, field.at[row, pl.ds(0, 2)], right.at[version, row + 2, pl.ds(0, 2)], ra, dec - 1),
        ]
        return ring, rightward, leftward

    def middle_copies(version):
        field = field_of(version)
        inner, own = pl.ds(2, rows - 4), pl.ds(4, rows - 4)
        return (
            copy(version, 20, field.at[inner, pl.ds(126, 2)], left.at[version, own, pl.ds(6, 2)], ra, dec + 1),
            copy(version, 21, field.at[inner, pl.ds(0, 2)], right.at[version, own, pl.ds(0, 2)], ra, dec - 1),
        )

    def start_row(version, toward, depth):
        ring, rightward, leftward = row_copies(version, toward, depth)

        @pl.when(has_right)
        def _():
            rightward[0].start()

        @pl.when(has_left)
        def _():
            leftward[0].start()

        ring.start()

        @pl.when(has_right)
        def _():
            rightward[1].start()

        @pl.when(has_left)
        def _():
            leftward[1].start()

    def start_middle(version):
        rightward, leftward = middle_copies(version)

        @pl.when(has_right)
        def _():
            rightward.start()

        @pl.when(has_left)
        def _():
            leftward.start()

    def receive_tips(version):
        middle = middle_copies(version)
        copies = [row_copies(version, toward, depth) for toward in range(2) for depth in range(2)]

        @pl.when(has_left)
        def _():
            for c in copies:
                c[1][1].wait_recv()
            middle[0].wait_recv()

        @pl.when(has_right)
        def _():
            for c in copies:
                c[2][1].wait_recv()
            middle[1].wait_recv()

    def receive_row(version, toward, depth):
        ring, rightward, leftward = row_copies(version, toward, depth)
        ring.wait_recv()

        @pl.when(has_left)
        def _():
            rightward[0].wait_recv()

        @pl.when(has_right)
        def _():
            leftward[0].wait_recv()

        place = (1 - depth) * (1 - toward) + (rows + 2 + depth) * toward
        put(version % 2, place, halo[version, toward, depth])
        put_tips(version, place)

    def finish_sends(version):
        middle = middle_copies(version)
        copies = [row_copies(version, toward, depth) for toward in range(2) for depth in range(2)]
        for c in copies:
            c[0].wait_send()

        @pl.when(has_right)
        def _():
            for c in copies:
                c[1][0].wait_send()
                c[1][1].wait_send()
            middle[0].wait_send()

        @pl.when(has_left)
        def _():
            for c in copies:
                c[2][0].wait_send()
                c[2][1].wait_send()
            middle[1].wait_send()

    def put(turn, place, value):
        first, second, third = three_parts(value)
        wide[turn, place, :, 0:128] = first
        wide[turn, place, :, 128:256] = second
        thin[turn, place] = third

    def put_tips(version, place):
        tips = jnp.concatenate([left[version, place], right[version, place]], axis=0)
        first, second, third = three_parts(tips)
        wide_halo[place, :, 0:128] = first
        wide_halo[place, :, 128:256] = second
        thin_halo[place, :, 0:128] = third

    for depth in range(2):
        for toward in (1 - near, near):
            start_row(0, toward, depth)
    start_middle(0)

    for version in range(STEPS):
        for place in range(rows + 4):
            left[version, place, 0:6] = jnp.zeros((6, 128), F32)
            right[version, place, 2:8] = jnp.zeros((6, 128), F32)

        @pl.when(dec == 0)
        def _():
            left[version] = jnp.zeros_like(left[version])

        @pl.when(dec == dec_count - 1)
        def _():
            right[version] = jnp.zeros_like(right[version])

    thin_halo[:, :, 128:256] = jnp.zeros((rows + 4, 16, 128), BF16)
    load_offsets.wait()
    load_degrees.wait()
    turned = jnp.transpose(degrees[...].astype(F32))
    for row in range(rows):
        degree_cols[row] = jnp.broadcast_to(turned[:, row : row + 1], (128, 128)) - 8.0

    load_edges.wait()

    def prepare(row, carry):
        put(0, row + 2, start[row])
        blank = jnp.zeros((6, 128), F32)
        tips = []
        for k in range(4):
            piece = raw_edges[row, pl.ds(8 + k, 128, 4), :].T
            first = piece.astype(BF16)
            place = slice(128 * k, 128 * k + 128)
            edge_pair[row, 0:128, place] = first
            edge_pair[row, 128:256, place] = (piece - first.astype(F32)).astype(BF16)
            tips += [blank] + [raw_edges[row, 4 * q + k : 4 * q + k + 1, :] for q in (0, 1, 130, 131)] + [blank]
        piece = jnp.concatenate(tips, axis=0).T
        first = piece.astype(BF16)
        second = (piece - first.astype(F32)).astype(BF16)
        edge_pair[row, 0:128, 512:640] = jnp.concatenate([first, first], axis=1)
        edge_pair[row, 128:256, 512:640] = jnp.concatenate([second, jnp.zeros_like(second)], axis=1)
        return carry

    lax.fori_loop(0, rows, prepare, 0)

    def one_row(version, row):
        turn = version % 2
        places = [row + offsets[k, row] for k in range(4)]
        both = jnp.concatenate(
            [wide[turn, p] for p in places] + [wide_halo[p] for p in places] + [thin_halo[p] for p in places], axis=0
        )
        last = jnp.concatenate([thin[turn, p] for p in places], axis=0)
        square = jnp.dot(edge_pair[row], both, preferred_element_type=F32)
        small = jnp.dot(edge_pair[row, 0:128, 0:512], last, preferred_element_type=F32)
        small = square[128:256, 128:256] + small
        coupled = square[0:128, 0:128] + ((square[0:128, 128:256] + square[128:256, 0:128]) + small)
        field = start[row] if version == 0 else fields[version - 1, row]
        image = degree_cols[row] * field - coupled
        if version == 0:
            return image * 0.25
        before = start[row] if version == 1 else fields[version - 2, row]
        return image * 0.5 - before

    def keep(version, row, value):
        if version == STEPS - 1:
            out[row] = value
        else:
            fields[version, row] = value
            put((version + 1) % 2, row + 2, value)

    def add_gram(values):
        gram_high, gram_low = local_gram(jnp.concatenate(values, axis=0))
        sums[0], error = two_sum(sums[0], gram_high)
        sums[1] = sums[1] + (gram_low + error)

    def run_pair(version, row):
        values = [one_row(version, row + i) for i in range(2)]
        for i, value in enumerate(values):
            keep(version, row + i, value)
        if version == STEPS - 1:
            add_gram(values)

    def run_edge(version, toward):
        outer, inner = (rows - 1) * (1 - toward), (rows - 2) * (1 - toward) + toward
        order = ((inner, 1), (outer, 0)) if version % 2 == 0 else ((outer, 0), (inner, 1))
        values = []
        for i, (row, depth) in enumerate(order):
            if version % 2 == 0:
                receive_row(version, 1 - toward, i)
            elif i == 0:
                receive_row(version, 1 - toward, 1)
                receive_row(version, 1 - toward, 0)
            values.append(one_row(version, row))
            keep(version, row, values[-1])
            if version < STEPS - 1:
                start_row(version + 1, toward, depth)
        if version == STEPS - 1:
            add_gram(values)

    sums[...] = jnp.zeros_like(sums)
    for version in range(STEPS):
        receive_tips(version)

        def tip(i, carry):
            put_tips(version, i + 2)
            return carry

        lax.fori_loop(0, rows, tip, 0)

        def interior(i, carry):
            run_pair(version, 2 * i + 2)
            return carry

        lax.fori_loop(0, (rows - 4) // 2, interior, 0)
        if version < STEPS - 1:
            start_middle(version + 1)

        def boundary(turn, carry):
            run_edge(version, turn + near - 2 * turn * near)
            return carry

        lax.fori_loop(0, 2, boundary, 0)

    save = pltpu.make_async_copy(out, filtered, edge_sem.at[0])
    save.start()
    for m in range(16):
        for half in range(2):
            part = pl.ds(8 * m + 4 * half, 4)
            tiles[2 * m + half, 0:4] = sums[0, part]
            tiles[2 * m + half, 4:8] = sums[1, part]
    sum_tiles(ra_count, dec_count, tiles, total, came, other, group_send, group_recv)
    save.wait()
    for version in range(STEPS):
        finish_sends(version)


def filtered_field(start_block, edges, offsets, degrees):
    rows = start_block.shape[0]
    vmem = pl.BlockSpec(memory_space=pltpu.VMEM)
    depth = 4 * 128 + 2 * HALO
    groups = group_count(lax.axis_size("ra"), lax.axis_size("dec"))
    return pl.pallas_call(
        functools.partial(filter_kernel, lax.axis_size("ra"), lax.axis_size("dec")),
        out_shape=(jax.ShapeDtypeStruct(start_block.shape, F32), jax.ShapeDtypeStruct((32, 8, 128), F32)),
        in_specs=[pl.BlockSpec(memory_space=pl.ANY)] * 4,
        out_specs=(pl.BlockSpec(memory_space=pl.ANY), vmem),
        scratch_shapes=[
            pltpu.SMEM(offsets.shape, jnp.int32),
            pltpu.VMEM(start_block.shape, F32),
            pltpu.VMEM(degrees.shape, jnp.int32),
            pltpu.VMEM(start_block.shape, F32),
            pltpu.VMEM((STEPS - 1, rows, 128, 128), F32),
            pltpu.VMEM((STEPS, 2, 2, 128, 128), F32),
            pltpu.VMEM((STEPS, rows + 4, 8, 128), F32),
            pltpu.VMEM((STEPS, rows + 4, 8, 128), F32),
            pltpu.VMEM((2, rows + 4, 128, 256), BF16),
            pltpu.VMEM((2, rows + 4, 128, 128), BF16),
            pltpu.VMEM((rows + 4, 16, 256), BF16),
            pltpu.VMEM((rows + 4, 16, 256), BF16),
            pltpu.VMEM(edges.shape, F32),
            pltpu.VMEM((rows, 256, depth), BF16),
            pltpu.VMEM((rows, 128, 128), F32),
            pltpu.VMEM((2, 128, 128), F32),
            pltpu.VMEM((32, 8, 128), F32),
            pltpu.VMEM((31, 8, 128), F32),
            pltpu.VMEM((groups, 8, 128), F32),
            pltpu.SemaphoreType.DMA((4,)),
            pltpu.SemaphoreType.DMA((STEPS, 22)),
            pltpu.SemaphoreType.DMA((STEPS, 22)),
            pltpu.SemaphoreType.DMA((3,)),
            pltpu.SemaphoreType.DMA((3,)),
        ],
        compiler_params=pltpu.CompilerParams(collective_id=0, has_side_effects=True, vmem_limit_bytes=60 * 2**20),
        name="filter",
    )(offsets, start_block, edges, degrees)


TILE = (8, 128)


def row_of(value, i):
    return jnp.broadcast_to(value[i : i + 1], TILE)


def factor(gram, side):
    sub = lax.broadcasted_iota(jnp.int32, TILE, 0)
    lane = lax.broadcasted_iota(jnp.int32, TILE, 1)
    blocks, panel = 16, 2
    width = 8 * panel
    body = [gram[8 * m : 8 * m + 8] for m in range(blocks)]
    side = [side[8 * m : 8 * m + 8] for m in range(blocks)]
    upper, inverse = [], []
    for begin in range(0, blocks, panel):
        end = begin + panel
        reach = min(blocks, end + panel)
        columns = {
            m: [jnp.broadcast_to(body[m][:, 8 * begin + j : 8 * begin + j + 1], TILE) for j in range(width)]
            for m in range(begin, reach)
        }
        for i in range(width):
            k, s = begin + i // 8, i % 8
            root = row_of(lax.rsqrt(columns[k][i]), s)
            entries = {j: row_of(columns[k][j], s) * root for j in range(i + 1, width)}
            for m in range(k, reach):
                columns[m][i] = columns[m][i] * root
                for j in range(i + 1, width):
                    columns[m][j] = columns[m][j] - columns[m][i] * entries[j]
            left_row, right_row = row_of(body[k], s) * root, row_of(side[k], s) * root
            upper_rows = left_row if s == 0 else jnp.where(sub == s, left_row, upper_rows)
            inverse_rows = right_row if s == 0 else jnp.where(sub == s, right_row, inverse_rows)
            for m in range(k if s < 7 else k + 1, reach):
                body[m] = body[m] - columns[m][i] * left_row
                side[m] = side[m] - columns[m][i] * right_row
            if s == 7:
                upper.append(jnp.where(lane >= sub + 8 * k, upper_rows, 0.0))
                inverse.append(jnp.where(lane <= sub + 8 * k, inverse_rows, 0.0))
        if reach < blocks:
            done = jnp.concatenate(upper[begin:end], axis=0)
            first, second, third = three_parts(jnp.concatenate([done, jnp.concatenate(inverse[begin:end], axis=0)], axis=1))
            parts = [p[:, 0:128].astype(F32) for p in (first, second, third)]
            turned = jnp.transpose(jnp.concatenate([parts[p] for p in (0, 0, 0, 1, 1, 2)], axis=0))[8 * reach :].astype(BF16)
            change = dot(turned, jnp.concatenate([first, second, third, first, second, first], axis=0))
            for m in range(reach, blocks):
                place = slice(8 * (m - reach), 8 * (m - reach) + 8)
                body[m] = body[m] - change[place, 0:128]
                side[m] = side[m] - change[place, 128:256]
    return jnp.concatenate(upper, axis=0), jnp.concatenate(inverse, axis=0)


def identity():
    shape = (128, 128)
    return jnp.where(lax.broadcasted_iota(jnp.int32, shape, 0) == lax.broadcasted_iota(jnp.int32, shape, 1), 1.0, 0.0).astype(F32)


def two_factors(high, low):
    first, inverse = factor(high, identity())
    parts = slices(first, 0, True)
    p = squares(dotT(jnp.concatenate(parts, axis=1), jnp.concatenate(parts[0:2], axis=1)))
    q = squares(dotT(jnp.concatenate(parts[0:3], axis=1), jnp.concatenate(parts[2:4], axis=1)))
    value, error = two_sum(high, -p[0][0])
    value, more = two_sum(value, -(p[0][1] + p[1][0]))
    value, last = two_sum(value, -(p[1][1] + (q[0][0] + p[2][0])))
    small = ((q[1][0] + p[2][1]) + (q[0][1] + p[3][0])) + (q[2][0] + (q[1][1] + p[3][1]))
    left_gram = value + (((low + error) + (more + last)) - small)

    p = squares(dotN(jnp.concatenate(slices(inverse, 1, True), axis=0), jnp.concatenate(slices(first, 1, True), axis=0)))
    left_inverse = (p[0][0] + (p[0][1] + p[1][0])) + (p[1][1] + (p[0][2] + p[2][0]))
    left_inverse = left_inverse + ((p[0][3] + p[3][0]) + (p[1][2] + p[2][1])) + ((p[2][2] + p[1][3]) + p[3][1]) - identity()

    turned = six_products(inverse, left_gram, (1, 0))
    gram_second = six_products(
        jnp.concatenate([turned, left_inverse], axis=1), jnp.concatenate([inverse, left_inverse], axis=1), (1, 1)
    )
    gram_second = identity() + (gram_second + (left_inverse + left_inverse.T))
    second, inverse = factor(gram_second, inverse)
    return six_products(second, first, (1, 0)), inverse


def finish_kernel(scale, gram, matrix, basis, rfactor):
    high = jnp.concatenate([gram[q, 0:4] for q in range(32)], axis=0)
    low = jnp.concatenate([gram[q, 4:8] for q in range(32)], axis=0)
    upper, inverse = two_factors(high, low)
    rfactor[...] = upper / scale
    basis[...] = six_products(matrix[...], inverse * scale, (1, 1))


def on_device(start_block, edge_blocks, block_offsets, degree_counts):
    edges = jnp.transpose(edge_blocks[:, 0], (0, 2, 1, 3)).reshape(start_block.shape[0], -1, 128)
    current, gram = filtered_field(start_block, edges, jnp.transpose(block_offsets[:, 0]), degree_counts)
    row_count, node_count, column_count = current.shape
    filtered = current.reshape(row_count * node_count, column_count)
    total_nodes = row_count * node_count * lax.axis_size("ra") * lax.axis_size("dec")
    scale = total_nodes**0.5
    vmem = pl.BlockSpec(memory_space=pltpu.VMEM)
    basis, rfactor = pl.pallas_call(
        functools.partial(finish_kernel, scale),
        out_shape=(jax.ShapeDtypeStruct(filtered.shape, F32), jax.ShapeDtypeStruct((128, 128), F32)),
        in_specs=[vmem] * 2,
        out_specs=(vmem,) * 2,
        name="finish",
    )(gram, filtered)
    return (basis.reshape(current.shape), rfactor)


def solution(mesh):
    placed = (
        P("ra", "dec", None),
        P("ra", "dec", None, None, None),
        P("ra", "dec", None),
        P("ra", "dec"),
    )
    return jax.shard_map(
        on_device,
        mesh=mesh,
        in_specs=placed,
        out_specs=(P("ra", "dec", None), P()),
        check_vma=False,
    )
```

```python
import functools

import jax
import jax.numpy as jnp
from jax import lax
from jax.experimental import pallas as pl
from jax.experimental.pallas import tpu as pltpu
from jax.sharding import PartitionSpec as P

MESH = pl.DeviceIdType.MESH
F32 = jnp.float32
BF16 = jnp.bfloat16
STEPS = 4
HALO = 64


def three_parts(value):
    first = value.astype(BF16)
    rest = value - first.astype(F32)
    second = rest.astype(BF16)
    third = (rest - second.astype(F32)).astype(BF16)
    return first, second, third


def dotT(a, b):
    return lax.dot_general(a, b, (((0,), (0,)), ((), ())), preferred_element_type=F32)


def dotN(a, b):
    return lax.dot_general(a, b, (((1,), (1,)), ((), ())), preferred_element_type=F32)


def dot(a, b):
    return jnp.dot(a, b, preferred_element_type=F32)

def two_sum(a, b):
    total = a + b
    other = total - a
    return total, (a - (total - other)) + (b - other)


def slices(value, axis, rest):
    shift = jnp.max(jnp.abs(value), axis=axis, keepdims=True) * (1.5 * 2.0**16)
    parts = []
    for _ in range(3):
        part = (value + shift) - shift
        value = value - part
        shift = shift * 2.0**-8
        parts.append(part.astype(BF16))
    return parts + [value.astype(BF16)] if rest else parts


def squares(matrix):
    return [
        [matrix[i : i + 128, j : j + 128] for j in range(0, matrix.shape[1], 128)] for i in range(0, matrix.shape[0], 128)
    ]


def local_gram(matrix):
    one, two, three = slices(matrix, 0, False)
    tall = jnp.concatenate([one, two, three], axis=1)
    p = squares(dotT(tall, jnp.concatenate([one, two], axis=1)))
    q = squares(dotT(tall, three))
    high, error = two_sum(p[0][0], p[0][1] + p[1][0])
    high, more = two_sum(high, p[1][1] + (q[0][0] + p[2][0]))
    return high, (error + more) + ((q[1][0] + p[2][1]) + q[2][0])


def six_products(a, b, dims):
    ah, am, al = three_parts(a)
    bh, bm, bl = three_parts(b)
    left = jnp.concatenate([ah, ah, ah, am, am, al], axis=dims[0])
    right = jnp.concatenate([bh, bm, bl, bh, bm, bh], axis=dims[1])
    return lax.dot_general(left, right, (((dims[0],), (dims[1],)), ((), ())), preferred_element_type=F32)


def group_rows(dec_count):
    return 32 // dec_count


def group_count(ra_count, dec_count):
    return ra_count // group_rows(dec_count)


def group_place(ra_count, dec_count):
    return lax.rem(lax.axis_index("ra"), group_rows(dec_count)) * dec_count + lax.axis_index("dec")


def group_partners(ra_count, dec_count):
    ra, dec = lax.axis_index("ra"), lax.axis_index("dec")
    place = group_place(ra_count, dec_count)
    flips = [2**bit - 2 ** (bit + 1) * lax.rem(lax.div(place, 2**bit), 2) for bit in range(5)]
    partners = []
    for step in range(1, 32):
        other, r, d = place, ra, dec
        for bit in range(5):
            if step >> bit & 1:
                other = other + flips[bit]
                if 2**bit < dec_count:
                    d = d + flips[bit]
                else:
                    r = r + lax.div(flips[bit], dec_count)
        partners.append((other, (r, d)))
    return partners


def other_partners(ra_count, dec_count):
    rows = group_rows(dec_count)
    return [
        (lax.rem(lax.axis_index("ra") + rows * step, ra_count), lax.axis_index("dec"))
        for step in range(1, group_count(ra_count, dec_count))
    ]


def spread_steps():
    return sorted(range(1, 32), key=lambda step: -sum((step >> bit & 1) << (4 - bit) for bit in range(5)))


def sum_tiles(ra_count, dec_count, tiles, total, came, other, send_sem, recv_sem):
    place = group_place(ra_count, dec_count)
    partners = group_partners(ra_count, dec_count)

    def copy(phase, source, target, device):
        return pltpu.make_async_remote_copy(
            src_ref=source, dst_ref=target, send_sem=send_sem.at[phase], recv_sem=recv_sem.at[phase],
            device_id=device, device_id_type=MESH,
        )

    def wait(semaphore, whole):
        pltpu.make_async_copy(whole, whole, semaphore).wait()

    def add(pieces):
        pairs = [(piece, jnp.zeros((8, 128), F32)) for piece in pieces]
        while len(pairs) > 1:
            merged = []
            for (a, e), (b, f) in zip(pairs[0::2], pairs[1::2]):
                value, more = two_sum(a, b)
                merged.append((value, more + (e + f)))
            pairs = merged + pairs[len(merged) * 2 :]
        value, error = pairs[0]
        high, low = two_sum(value[0:4], value[4:8] + (error[0:4] + error[4:8]))
        return jnp.concatenate([high, low], axis=0)

    for step in spread_steps():
        owner, device = partners[step - 1]
        copy(0, tiles.at[owner], came.at[step - 1], device).start()
    wait(recv_sem.at[0], came)
    value = add([tiles[place]] + [came[step - 1] for step in range(1, 32)])
    if group_count(ra_count, dec_count) > 1:
        other[0] = value
        for step, device in enumerate(other_partners(ra_count, dec_count), 1):
            copy(1, other.at[0], other.at[step], device).start()
        wait(recv_sem.at[1], other.at[pl.ds(1, group_count(ra_count, dec_count) - 1)])
        value = add([other[step] for step in range(group_count(ra_count, dec_count))])
        wait(send_sem.at[1], other.at[pl.ds(1, group_count(ra_count, dec_count) - 1)])
    total[place] = value
    for step in spread_steps():
        copy(2, total.at[place], total.at[place], partners[step - 1][1]).start()
    wait(recv_sem.at[2], came)
    wait(send_sem.at[0], came)
    wait(send_sem.at[2], came)


def filter_kernel(
    ra_count, dec_count, offsets_in, start_in, edges, degrees_in, filtered, total,
    offsets, start, degrees, out, fields, halo, left, right, wide, thin, wide_halo, thin_halo, raw_edges, edge_pair, degree_cols, sums,
    tiles, came, other, edge_sem, send_sem, recv_sem, group_send, group_recv,
):
    rows = start.shape[0]
    ra = lax.axis_index("ra")
    dec = lax.axis_index("dec")
    up = lax.rem(ra + 1, ra_count)
    down = lax.rem(ra + ra_count - 1, ra_count)
    has_left = dec > 0
    has_right = dec < dec_count - 1
    near = lax.rem(ra, 2)

    load_start = pltpu.make_async_copy(start_in, start, edge_sem.at[1])
    load_edges = pltpu.make_async_copy(edges, raw_edges, edge_sem.at[0])
    load_offsets = pltpu.make_async_copy(offsets_in, offsets, edge_sem.at[2])
    load_degrees = pltpu.make_async_copy(degrees_in, degrees, edge_sem.at[3])
    for c in (load_start, load_offsets, load_degrees, load_edges):
        c.start()
    barrier = pltpu.get_barrier_semaphore()

    def greet(r, d):
        pl.semaphore_signal(barrier, inc=1, device_id=(r, d), device_id_type=MESH)

    greet(up, dec)
    greet(down, dec)

    @pl.when(has_left)
    def _():
        for r in (up, down, ra):
            greet(r, dec - 1)

    @pl.when(has_right)
    def _():
        for r in (up, down, ra):
            greet(r, dec + 1)

    count = 2 + 3 * jnp.where(has_left, 1, 0) + 3 * jnp.where(has_right, 1, 0)
    if ra_count > 2 * STEPS or dec_count > STEPS:
        far = [device for _, device in group_partners(ra_count, dec_count)] + other_partners(ra_count, dec_count)
        for r, d in far:
            greet(r, d)
        count = count + len(far)
    load_start.wait()
    pl.semaphore_wait(barrier, count)

    def copy(version, slot, source, target, r, d):
        return pltpu.make_async_remote_copy(
            src_ref=source, dst_ref=target, send_sem=send_sem.at[version, slot], recv_sem=recv_sem.at[version, slot],
            device_id=(r, d), device_id_type=MESH,
        )

    def field_of(version):
        return start if version == 0 else fields.at[version - 1]

    def row_copies(version, toward, depth):
        field = field_of(version)
        row = (rows - 1 - depth) * (1 - toward) + depth * toward
        target = up * (1 - toward) + down * toward
        corner = (1 - depth) * (1 - toward) + (rows + 2 + depth) * toward
        slot = 10 * toward + 5 * depth
        ring = copy(version, slot, field.at[row], halo.at[version, toward, depth], target, dec)
        rightward = [
            copy(version, slot + 1, field.at[row, pl.ds(126, 2)], left.at[version, corner, pl.ds(6, 2)], target, dec + 1),
            copy(version, slot + 2, field.at[row, pl.ds(126, 2)], left.at[version, row + 2, pl.ds(6, 2)], ra, dec + 1),
        ]
        leftward = [
            copy(version, slot + 3, field.at[row, pl.ds(0, 2)], right.at[version, corner, pl.ds(0, 2)], target, dec - 1),
            copy(version, slot + 4, field.at[row, pl.ds(0, 2)], right.at[version, row + 2, pl.ds(0, 2)], ra, dec - 1),
        ]
        return ring, rightward, leftward

    def middle_copies(version):
        field = field_of(version)
        inner, own = pl.ds(2, rows - 4), pl.ds(4, rows - 4)
        return (
            copy(version, 20, field.at[inner, pl.ds(126, 2)], left.at[version, own, pl.ds(6, 2)], ra, dec + 1),
            copy(version, 21, field.at[inner, pl.ds(0, 2)], right.at[version, own, pl.ds(0, 2)], ra, dec - 1),
        )

    def start_row(version, toward, depth):
        ring, rightward, leftward = row_copies(version, toward, depth)

        @pl.when(has_right)
        def _():
            rightward[0].start()

        @pl.when(has_left)
        def _():
            leftward[0].start()

        ring.start()

        @pl.when(has_right)
        def _():
            rightward[1].start()

        @pl.when(has_left)
        def _():
            leftward[1].start()

    def start_middle(version):
        rightward, leftward = middle_copies(version)

        @pl.when(has_right)
        def _():
            rightward.start()

        @pl.when(has_left)
        def _():
            leftward.start()

    def receive_tips(version):
        middle = middle_copies(version)
        copies = [row_copies(version, toward, depth) for toward in range(2) for depth in range(2)]

        @pl.when(has_left)
        def _():
            for c in copies:
                c[1][1].wait_recv()
            middle[0].wait_recv()

        @pl.when(has_right)
        def _():
            for c in copies:
                c[2][1].wait_recv()
            middle[1].wait_recv()

    def receive_row(version, toward, depth):
        ring, rightward, leftward = row_copies(version, toward, depth)
        ring.wait_recv()

        @pl.when(has_left)
        def _():
            rightward[0].wait_recv()

        @pl.when(has_right)
        def _():
            leftward[0].wait_recv()

        place = (1 - depth) * (1 - toward) + (rows + 2 + depth) * toward
        put(version % 2, place, halo[version, toward, depth])
        put_tips(version, place)

    def finish_sends(version):
        middle = middle_copies(version)
        copies = [row_copies(version, toward, depth) for toward in range(2) for depth in range(2)]
        for c in copies:
            c[0].wait_send()

        @pl.when(has_right)
        def _():
            for c in copies:
                c[1][0].wait_send()
                c[1][1].wait_send()
            middle[0].wait_send()

        @pl.when(has_left)
        def _():
            for c in copies:
                c[2][0].wait_send()
                c[2][1].wait_send()
            middle[1].wait_send()

    def put(turn, place, value):
        first, second, third = three_parts(value)
        wide[turn, place, :, 0:128] = first
        wide[turn, place, :, 128:256] = second
        thin[turn, place] = third

    def put_tips(version, place):
        tips = jnp.concatenate([left[version, place], right[version, place]], axis=0)
        first, second, third = three_parts(tips)
        wide_halo[place, :, 0:128] = first
        wide_halo[place, :, 128:256] = second
        thin_halo[place, :, 0:128] = third

    for depth in range(2):
        for toward in (1 - near, near):
            start_row(0, toward, depth)
    start_middle(0)

    for version in range(STEPS):
        for place in range(rows + 4):
            left[version, place, 0:6] = jnp.zeros((6, 128), F32)
            right[version, place, 2:8] = jnp.zeros((6, 128), F32)

        @pl.when(dec == 0)
        def _():
            left[version] = jnp.zeros_like(left[version])

        @pl.when(dec == dec_count - 1)
        def _():
            right[version] = jnp.zeros_like(right[version])

    thin_halo[:, :, 128:256] = jnp.zeros((rows + 4, 16, 128), BF16)
    load_offsets.wait()
    load_degrees.wait()
    turned = jnp.transpose(degrees[...].astype(F32))
    for row in range(rows):
        degree_cols[row] = jnp.broadcast_to(turned[:, row : row + 1], (128, 128)) - 8.0

    load_edges.wait()

    def prepare(row, carry):
        put(0, row + 2, start[row])
        blank = jnp.zeros((6, 128), F32)
        tips = []
        for k in range(4):
            piece = raw_edges[row, pl.ds(8 + k, 128, 4), :].T
            first = piece.astype(BF16)
            place = slice(128 * k, 128 * k + 128)
            edge_pair[row, 0:128, place] = first
            edge_pair[row, 128:256, place] = (piece - first.astype(F32)).astype(BF16)
            tips += [blank] + [raw_edges[row, 4 * q + k : 4 * q + k + 1, :] for q in (0, 1, 130, 131)] + [blank]
        piece = jnp.concatenate(tips, axis=0).T
        first = piece.astype(BF16)
        second = (piece - first.astype(F32)).astype(BF16)
        edge_pair[row, 0:128, 512:640] = jnp.concatenate([first, first], axis=1)
        edge_pair[row, 128:256, 512:640] = jnp.concatenate([second, jnp.zeros_like(second)], axis=1)
        return carry

    lax.fori_loop(0, rows, prepare, 0)

    def one_row(version, row):
        turn = version % 2
        places = [row + offsets[k, row] for k in range(4)]
        both = jnp.concatenate(
            [wide[turn, p] for p in places] + [wide_halo[p] for p in places] + [thin_halo[p] for p in places], axis=0
        )
        last = jnp.concatenate([thin[turn, p] for p in places], axis=0)
        square = jnp.dot(edge_pair[row], both, preferred_element_type=F32)
        small = jnp.dot(edge_pair[row, 0:128, 0:512], last, preferred_element_type=F32)
        small = square[128:256, 128:256] + small
        coupled = square[0:128, 0:128] + ((square[0:128, 128:256] + square[128:256, 0:128]) + small)
        field = start[row] if version == 0 else fields[version - 1, row]
        image = degree_cols[row] * field - coupled
        if version == 0:
            return image * 0.25
        before = start[row] if version == 1 else fields[version - 2, row]
        return image * 0.5 - before

    def keep(version, row, value):
        if version == STEPS - 1:
            out[row] = value
        else:
            fields[version, row] = value
            put((version + 1) % 2, row + 2, value)

    def add_gram(values):
        gram_high, gram_low = local_gram(jnp.concatenate(values, axis=0))
        sums[0], error = two_sum(sums[0], gram_high)
        sums[1] = sums[1] + (gram_low + error)

    def run_pair(version, row):
        values = [one_row(version, row + i) for i in range(2)]
        for i, value in enumerate(values):
            keep(version, row + i, value)
        if version == STEPS - 1:
            add_gram(values)

    def run_edge(version, toward):
        outer, inner = (rows - 1) * (1 - toward), (rows - 2) * (1 - toward) + toward
        order = ((inner, 1), (outer, 0)) if version % 2 == 0 else ((outer, 0), (inner, 1))
        values = []
        for i, (row, depth) in enumerate(order):
            if version % 2 == 0:
                receive_row(version, 1 - toward, i)
            elif i == 0:
                receive_row(version, 1 - toward, 1)
                receive_row(version, 1 - toward, 0)
            values.append(one_row(version, row))
            keep(version, row, values[-1])
            if version < STEPS - 1:
                start_row(version + 1, toward, depth)
        if version == STEPS - 1:
            add_gram(values)

    sums[...] = jnp.zeros_like(sums)
    for version in range(STEPS):
        receive_tips(version)

        def tip(i, carry):
            put_tips(version, i + 2)
            return carry

        lax.fori_loop(0, rows, tip, 0)

        def interior(i, carry):
            run_pair(version, 2 * i + 2)
            return carry

        lax.fori_loop(0, (rows - 4) // 2, interior, 0)
        if version < STEPS - 1:
            start_middle(version + 1)

        def boundary(turn, carry):
            run_edge(version, turn + near - 2 * turn * near)
            return carry

        lax.fori_loop(0, 2, boundary, 0)

    save = pltpu.make_async_copy(out, filtered, edge_sem.at[0])
    save.start()
    for m in range(16):
        for half in range(2):
            part = pl.ds(8 * m + 4 * half, 4)
            tiles[2 * m + half, 0:4] = sums[0, part]
            tiles[2 * m + half, 4:8] = sums[1, part]
    sum_tiles(ra_count, dec_count, tiles, total, came, other, group_send, group_recv)
    save.wait()
    for version in range(STEPS):
        finish_sends(version)


def filtered_field(start_block, edges, offsets, degrees):
    rows = start_block.shape[0]
    vmem = pl.BlockSpec(memory_space=pltpu.VMEM)
    depth = 4 * 128 + 2 * HALO
    groups = group_count(lax.axis_size("ra"), lax.axis_size("dec"))
    return pl.pallas_call(
        functools.partial(filter_kernel, lax.axis_size("ra"), lax.axis_size("dec")),
        out_shape=(jax.ShapeDtypeStruct(start_block.shape, F32), jax.ShapeDtypeStruct((32, 8, 128), F32)),
        in_specs=[pl.BlockSpec(memory_space=pl.ANY)] * 4,
        out_specs=(pl.BlockSpec(memory_space=pl.ANY), vmem),
        scratch_shapes=[
            pltpu.SMEM(offsets.shape, jnp.int32),
            pltpu.VMEM(start_block.shape, F32),
            pltpu.VMEM(degrees.shape, jnp.int32),
            pltpu.VMEM(start_block.shape, F32),
            pltpu.VMEM((STEPS - 1, rows, 128, 128), F32),
            pltpu.VMEM((STEPS, 2, 2, 128, 128), F32),
            pltpu.VMEM((STEPS, rows + 4, 8, 128), F32),
            pltpu.VMEM((STEPS, rows + 4, 8, 128), F32),
            pltpu.VMEM((2, rows + 4, 128, 256), BF16),
            pltpu.VMEM((2, rows + 4, 128, 128), BF16),
            pltpu.VMEM((rows + 4, 16, 256), BF16),
            pltpu.VMEM((rows + 4, 16, 256), BF16),
            pltpu.VMEM(edges.shape, F32),
            pltpu.VMEM((rows, 256, depth), BF16),
            pltpu.VMEM((rows, 128, 128), F32),
            pltpu.VMEM((2, 128, 128), F32),
            pltpu.VMEM((32, 8, 128), F32),
            pltpu.VMEM((31, 8, 128), F32),
            pltpu.VMEM((groups, 8, 128), F32),
            pltpu.SemaphoreType.DMA((4,)),
            pltpu.SemaphoreType.DMA((STEPS, 22)),
            pltpu.SemaphoreType.DMA((STEPS, 22)),
            pltpu.SemaphoreType.DMA((3,)),
            pltpu.SemaphoreType.DMA((3,)),
        ],
        compiler_params=pltpu.CompilerParams(collective_id=0, has_side_effects=True, vmem_limit_bytes=60 * 2**20),
        name="filter",
    )(offsets, start_block, edges, degrees)


TILE = (8, 128)


def row_of(value, i):
    return jnp.broadcast_to(value[i : i + 1], TILE)


def factor(gram, side):
    sub = lax.broadcasted_iota(jnp.int32, TILE, 0)
    lane = lax.broadcasted_iota(jnp.int32, TILE, 1)
    blocks, panel = 16, 2
    width = 8 * panel
    body = [gram[8 * m : 8 * m + 8] for m in range(blocks)]
    side = [side[8 * m : 8 * m + 8] for m in range(blocks)]
    upper, inverse = [], []
    for begin in range(0, blocks, panel):
        end = begin + panel
        reach = min(blocks, end + panel)
        columns = {
            m: [jnp.broadcast_to(body[m][:, 8 * begin + j : 8 * begin + j + 1], TILE) for j in range(width)]
            for m in range(begin, reach)
        }
        for i in range(width):
            k, s = begin + i // 8, i % 8
            root = row_of(lax.rsqrt(columns[k][i]), s)
            entries = {j: row_of(columns[k][j], s) * root for j in range(i + 1, width)}
            for m in range(k, reach):
                columns[m][i] = columns[m][i] * root
                for j in range(i + 1, width):
                    columns[m][j] = columns[m][j] - columns[m][i] * entries[j]
            left_row, right_row = row_of(body[k], s) * root, row_of(side[k], s) * root
            upper_rows = left_row if s == 0 else jnp.where(sub == s, left_row, upper_rows)
            inverse_rows = right_row if s == 0 else jnp.where(sub == s, right_row, inverse_rows)
            for m in range(k if s < 7 else k + 1, reach):
                body[m] = body[m] - columns[m][i] * left_row
                side[m] = side[m] - columns[m][i] * right_row
            if s == 7:
                upper.append(jnp.where(lane >= sub + 8 * k, upper_rows, 0.0))
                inverse.append(jnp.where(lane <= sub + 8 * k, inverse_rows, 0.0))
        if reach < blocks:
            done = jnp.concatenate(upper[begin:end], axis=0)
            first, second, third = three_parts(jnp.concatenate([done, jnp.concatenate(inverse[begin:end], axis=0)], axis=1))
            parts = [p[:, 0:128].astype(F32) for p in (first, second, third)]
            turned = jnp.transpose(jnp.concatenate([parts[p] for p in (0, 0, 0, 1, 1, 2)], axis=0))[8 * reach :].astype(BF16)
            change = dot(turned, jnp.concatenate([first, second, third, first, second, first], axis=0))
            for m in range(reach, blocks):
                place = slice(8 * (m - reach), 8 * (m - reach) + 8)
                body[m] = body[m] - change[place, 0:128]
                side[m] = side[m] - change[place, 128:256]
    return jnp.concatenate(upper, axis=0), jnp.concatenate(inverse, axis=0)


def identity():
    shape = (128, 128)
    return jnp.where(lax.broadcasted_iota(jnp.int32, shape, 0) == lax.broadcasted_iota(jnp.int32, shape, 1), 1.0, 0.0).astype(F32)


def two_factors(high, low):
    first, inverse = factor(high, identity())
    parts = slices(first, 0, True)
    p = squares(dotT(jnp.concatenate(parts, axis=1), jnp.concatenate(parts[0:2], axis=1)))
    q = squares(dotT(jnp.concatenate(parts[0:3], axis=1), jnp.concatenate(parts[2:4], axis=1)))
    value, error = two_sum(high, -p[0][0])
    value, more = two_sum(value, -(p[0][1] + p[1][0]))
    value, last = two_sum(value, -(p[1][1] + (q[0][0] + p[2][0])))
    small = ((q[1][0] + p[2][1]) + (q[0][1] + p[3][0])) + (q[2][0] + (q[1][1] + p[3][1]))
    left_gram = value + (((low + error) + (more + last)) - small)

    p = squares(dotN(jnp.concatenate(slices(inverse, 1, True), axis=0), jnp.concatenate(slices(first, 1, True), axis=0)))
    left_inverse = (p[0][0] + (p[0][1] + p[1][0])) + (p[1][1] + (p[0][2] + p[2][0]))
    left_inverse = left_inverse + ((p[0][3] + p[3][0]) + (p[1][2] + p[2][1])) + ((p[2][2] + p[1][3]) + p[3][1]) - identity()

    turned = six_products(inverse, left_gram, (1, 0))
    gram_second = six_products(
        jnp.concatenate([turned, left_inverse], axis=1), jnp.concatenate([inverse, left_inverse], axis=1), (1, 1)
    )
    gram_second = identity() + (gram_second + (left_inverse + left_inverse.T))
    second, inverse = factor(gram_second, inverse)
    return six_products(second, first, (1, 0)), inverse


def finish_kernel(scale, gram, matrix, basis, rfactor):
    high = jnp.concatenate([gram[q, 0:4] for q in range(32)], axis=0)
    low = jnp.concatenate([gram[q, 4:8] for q in range(32)], axis=0)
    upper, inverse = two_factors(high, low)
    rfactor[...] = upper / scale
    basis[...] = six_products(matrix[...], inverse * scale, (1, 1))


def on_device(start_block, edge_blocks, block_offsets, degree_counts):
    edges = jnp.transpose(edge_blocks[:, 0], (0, 2, 1, 3)).reshape(start_block.shape[0], -1, 128)
    current, gram = filtered_field(start_block, edges, jnp.transpose(block_offsets[:, 0]), degree_counts)
    row_count, node_count, column_count = current.shape
    filtered = current.reshape(row_count * node_count, column_count)
    total_nodes = row_count * node_count * lax.axis_size("ra") * lax.axis_size("dec")
    scale = total_nodes**0.5
    vmem = pl.BlockSpec(memory_space=pltpu.VMEM)
    basis, rfactor = pl.pallas_call(
        functools.partial(finish_kernel, scale),
        out_shape=(jax.ShapeDtypeStruct(filtered.shape, F32), jax.ShapeDtypeStruct((128, 128), F32)),
        in_specs=[vmem] * 2,
        out_specs=(vmem,) * 2,
        name="finish",
    )(gram, filtered)
    return (basis.reshape(current.shape), rfactor)


def solution(mesh):
    placed = (
        P("ra", "dec", None),
        P("ra", "dec", None, None, None),
        P("ra", "dec", None),
        P("ra", "dec"),
    )
    return jax.shard_map(
        on_device,
        mesh=mesh,
        in_specs=placed,
        out_specs=(P("ra", "dec", None), P()),
        check_vma=False,
    )
```
